512 devices in a mesh: star: 16 (over y, core), cad: 32 (over z, x).
Axes of the slice: x: 4, y: 8, z: 8, core: 2. Of those that a mesh axis runs over, the one named last changes fastest.
Arguments:
- light: float32 [65536, 8192], P('star', 'cad'), may hold values from -2000 to 2000
- quality: int32 [8192], P('cad'), may hold values 0 or 1
- star_factors: float32 [65536, 128], P('star', 'cad'), may hold values from -6 to 6
- cadence_factors: float32 [8192, 128], P('cad', 'star'), may hold values from -6 to 6
Outputs:
- star_gradient: float32 [65536, 128], P('star', 'cad')
- cadence_gradient: float32 [8192, 128], P('cad', 'star')
- loss: float32 [], replicated
The draws below stay inside these ranges and needn't reach their ends.
All inputs are finite; a program needn't handle non-finite values. No bound on the sum of `quality` on one device may be relied on, other than what follows from the above.
Results may differ from the reference program's by a relative error of at most 0.0003.
Values sent between devices are 32-bit elements; how exact they have to be, the bound alone decides.
A program may use at most 64 MiB of HBM per device.

```python
import jax
import jax.numpy as jnp
from jax import lax

RANK = 128
STARS = 65536
CADS = 8192


def draw_light(key, part):
    keys = jax.random.split(key, 6)
    star_pos = jnp.arange(STARS, dtype=jnp.float32)[:, None] / STARS
    row_scale = jnp.exp(jnp.log(10.0) * star_pos + 0.5 * jax.random.uniform(keys[1], (STARS, 1), jnp.float32))
    col_scale = jnp.exp(jnp.log(4.0) * jax.random.uniform(keys[2], (1, CADS), jnp.float32))
    period = jax.random.randint(keys[3], (STARS, 1), 40, 400)
    phase = jax.random.randint(keys[4], (STARS, 1), 0, 400)
    cadence = jnp.arange(CADS, dtype=jnp.int32)[None, :]
    transit = ((cadence + phase) % period < 12).astype(jnp.float32)
    depth = jax.random.uniform(keys[5], (STARS, 1), jnp.float32, 1.0, 4.0)
    noise = jax.random.normal(keys[0], (STARS, CADS), jnp.float32)
    noise = jnp.clip(noise, -6.0, 6.0)
    values = row_scale * (col_scale * noise - depth * transit)
    return values.astype(jnp.float32)


def plant(array, own_key, low, high):
    index_at = [jax.random.randint(jax.random.fold_in(own_key, axis), (), 0, length) for axis, length in enumerate(array.shape)]
    main_axis = array.shape.index(max(array.shape))
    next_to = index_at[:main_axis] + [(index_at[main_axis] + 1) % array.shape[main_axis]] + index_at[main_axis + 1:]
    return array.at[tuple(index_at)].set(low).at[tuple(next_to)].set(high)


def level_of(stream_key, shape, cuts, low, largest):
    factor_of = 1.0
    for position, blocks in cuts:
        draws = jax.random.uniform(jax.random.fold_in(jax.random.fold_in(stream_key, 6), position), (blocks,), jnp.float32, low / len(cuts), largest / len(cuts))
        factor_of = factor_of * jnp.repeat(jnp.exp(draws), shape[position] // blocks).reshape((-1,) + (1,) * (len(shape) - 1 - position))
    return factor_of


def scatter_about(rng, dims, scale, bound, cuts=(), kind=jnp.bfloat16):
    values = scale * jax.random.normal(rng, dims, jnp.float32)
    if cuts:
        values = values * level_of(rng, dims, cuts, -0.22, 0.18)
    return jnp.clip(values, -bound, bound).astype(kind)


def setup_inputs(seed: int = 0) -> dict:
    key_of = jax.random.split(jax.random.key(seed), 5)
    light = draw_light(jax.random.fold_in(key_of[4], 71), 0)
    quality = plant((jax.random.randint(key_of[1], (CADS,), 0, 8) < 7).astype(jnp.int32), jax.random.fold_in(key_of[1], 1), 0, 1)
    star_factors = scatter_about(key_of[2], (STARS, RANK), 1.0, 6.0, ((0, 16), (1, 32)), jnp.float32)
    cadence_factors = scatter_about(key_of[3], (CADS, RANK), 1.0, 6.0, ((0, 32), (1, 16)), jnp.float32)
    return dict(light=light, quality=quality, star_factors=star_factors, cadence_factors=cadence_factors)


def reference(light, quality, star_factors, cadence_factors):
    total_stars = light.shape[0]
    total_cads = light.shape[1]
    block = min(4096, total_stars)
    count = total_stars // block
    good = quality.astype(jnp.float32)[None, :]
    light_blocks = light.reshape(count, block, total_cads)
    factor_blocks = star_factors.reshape(count, block, star_factors.shape[1])

    def one_block(carry, pieces):
        cad_sum, loss_sum = carry
        rows, loads = pieces
        predicted = jnp.dot(loads, cadence_factors.T, precision=lax.Precision.HIGHEST, preferred_element_type=jnp.float32)
        residual = rows - predicted
        ratio = 1.0 + (residual * 0.5) ** 2
        weighted = good * residual / ratio
        star_part = -jnp.dot(weighted, cadence_factors, precision=lax.Precision.HIGHEST, preferred_element_type=jnp.float32) / jnp.sqrt(jnp.float32(total_cads))
        cad_sum = cad_sum + jnp.dot(weighted.T, loads, precision=lax.Precision.HIGHEST, preferred_element_type=jnp.float32)
        loss_sum = loss_sum + jnp.sum(good * 2.0 * jnp.log(ratio))
        return ((cad_sum, loss_sum), star_part)
    start = (jnp.zeros(cadence_factors.shape, jnp.float32), jnp.zeros((), jnp.float32))
    (cad_sum, loss_sum), star_parts = lax.scan(one_block, start, (light_blocks, factor_blocks))
    star_gradient = star_parts.reshape(star_factors.shape)
    cadence_gradient = -cad_sum / jnp.sqrt(jnp.float32(total_stars))
    loss = loss_sum / (jnp.float32(total_stars) * jnp.float32(total_cads))
    return (star_gradient, cadence_gradient, loss)
```

```python
import functools

import jax
import jax.numpy as jnp
from jax import lax
from jax.experimental import pallas as pl
from jax.experimental.pallas import tpu as pltpu
from jax.sharding import PartitionSpec as P

MESH = pl.DeviceIdType.MESH
F32, BF16 = jnp.float32, jnp.bfloat16
NZ, NX, NY = 8, 4, 8
HALF = 2048
CADS = 256
BLOCK = 256
CHUNKS = (("xz", 0, 512), ("zx", 512, 512), ("xz", 1024, 512), ("zx", 1536, 512))
MESSAGES = 10


def split(value):
    high = value.astype(BF16)
    return high, (value - high.astype(F32)).astype(BF16)


def dot3(a, b, dims):
    def one(p, q):
        return lax.dot_general(p, q, (dims, ((), ())), preferred_element_type=F32)

    return one(a[0], b[0]) + (one(a[0], b[1]) + one(a[1], b[0]))


def kernel(
    star_scale, cad_scale, loss_scale,
    light_ref, quality_ref, star_ref, cad_ref,
    star_out, cad_out, loss_out,
    light, own, slabs, grads, cads, expanded, wide_high, wide_low, good, acc, logs,
    cad_part, cad_core, cad_from, loss_x, loss_z, *rest,
):
    boxes, (sems, gather_send, gather_recv, reduce_send, reduce_recv, small_send, small_recv) = rest[:-7], rest[-7:]
    star, cad = lax.axis_index("star"), lax.axis_index("cad")
    y, core = star // 2, lax.rem(star, 2)
    z, x = cad // NX, lax.rem(cad, NX)

    def at_z(d):
        return lax.rem(z + d + NZ, NZ)

    def at_x(d):
        return lax.rem(x + d + NX, NX)

    def at_y(d):
        return lax.rem(y + d, NY)

    def to_z(d):
        return (star, at_z(d) * NX + x)

    def to_x(d):
        return (star, z * NX + at_x(d))

    def to_y(d):
        return (at_y(d) * 2 + core, cad)

    partner = (y * 2 + 1 - core, cad)

    light_copy = pltpu.make_async_copy(light_ref, light, sems.at[0])
    own_copy = pltpu.make_async_copy(star_ref, own, sems.at[1])
    cad_copy = pltpu.make_async_copy(cad_ref, cads.at[y, core], sems.at[2])
    good_copy = pltpu.make_async_copy(quality_ref, good, sems.at[3])
    own_copy.start()
    cad_copy.start()
    good_copy.start()

    barrier = pltpu.get_barrier_semaphore()
    peers = [to_z(d) for d in range(1, NZ)] + [to_x(d) for d in range(1, NX)]
    peers += [to_y(d) for d in range(1, NY)] + [partner]
    for peer in peers:
        pl.semaphore_signal(barrier, inc=1, device_id=peer, device_id_type=MESH)
    own_copy.wait()
    slabs[z, x, 0:4, :] = own[:, :HALF]
    slabs[z, x, 4:8, :] = own[:, HALF:]
    pl.semaphore_wait(barrier, len(peers))

    def remote(src, dst, send, recv, where):
        copy = pltpu.make_async_remote_copy(
            src_ref=src, dst_ref=dst, send_sem=send, recv_sem=recv,
            device_id=where, device_id_type=MESH,
        )
        copy.start()
        return copy

    sent = []

    def gather_rounds(index, order, first, width):
        columns = pl.ds(first, width)
        count = [0]

        def view(ref, axis, place):
            if axis == order[0]:
                return ref.at[(place, x) if axis == "z" else (z, place)].at[:, columns]
            if axis == "z":
                return ref.at[place].at[:, :, columns]
            return ref.at[:, place].at[:, :, columns]

        def send(axis, origin, step):
            block = view(slabs, axis, origin)
            n = index * MESSAGES + count[0]
            count[0] += 1
            where = to_z(step) if axis == "z" else to_x(step)
            copy = remote(block, block, gather_send.at[n], gather_recv.at[n], where)
            sent.append(copy)
            return copy

        up = {}
        odd = index // 2 % 2
        for axis in order:
            at, size = (at_z, NZ) if axis == "z" else (at_x, NX)
            right, left = send(axis, at(0), 1), send(axis, at(0), -1)
            yield
            for hop in range(1, size // 2):
                last = hop == size // 2 - 1
                right.wait_recv()
                if not last or not odd:
                    right_next = send(axis, at(-hop), 1)
                left.wait_recv()
                if not last or odd:
                    left = send(axis, at(hop), -1)
                if not last or not odd:
                    right = right_next
                yield
            (left if odd else right).wait_recv()

    def reduce_rounds(index, order, first, width, box_far, box_near):
        columns = pl.ds(first, width)
        count = [0]

        def view(axis, place):
            if axis == order[0]:
                return grads.at[(place, x) if axis == "z" else (z, place)].at[:, columns]
            if axis == "z":
                return grads.at[place].at[:, :, columns]
            return grads.at[:, place].at[:, :, columns]

        odd = index // 2 % 2
        for axis, box in ((order[1], box_far), (order[0], box_near)):
            at, size = (at_z, NZ) if axis == "z" else (at_x, NX)
            far = size // 2
            slot = [0]

            def send(owner, step):
                n = index * MESSAGES + count[0]
                count[0] += 1
                where = to_z(step) if axis == "z" else to_x(step)
                landing = box.at[slot[0]]
                slot[0] += 1
                copy = remote(view(axis, owner), landing, reduce_send.at[n], reduce_recv.at[n], where)
                sent.append(copy)
                return copy, landing

            def take(arrived, owner):
                arrived[0].wait_recv()
                mine = view(axis, owner)
                mine[...] = mine[...] + arrived[1][...]

            sign = 1 if odd else -1
            long = send(at(sign * far), sign)
            short = send(at(-sign * (far - 1)), -sign)
            yield
            for hop in range(1, far):
                take(long, at(sign * (far - hop)))
                long = send(at(sign * (far - hop)), sign)
                if hop < far - 1:
                    take(short, at(-sign * (far - 1 - hop)))
                    short = send(at(-sign * (far - 1 - hop)), -sign)
                yield
            take(short, at(0))
            take(long, at(0))

    cad_copy.wait()
    cad_in = [
        remote(cads.at[y, core], cads.at[y, core], small_send.at[d - 1], small_recv.at[d - 1], to_y(d))
        for d in range(1, NY)
    ]
    sent.extend(cad_in)
    gathers = [gather_rounds(i, *chunk) for i, chunk in enumerate(CHUNKS)]
    for g in gathers:
        next(g)
    light_copy.start()
    for g in gathers:
        next(g)
    for copy in cad_in:
        copy.wait_recv()
    cad_across = remote(cads.at[:, core], cads.at[:, core], small_send.at[7], small_recv.at[7], partner)
    sent.append(cad_across)
    for g in gathers:
        next(g)
    cad_across.wait_recv()

    good_copy.wait()
    keep = good[...].astype(F32)
    values = cads[...].reshape(16, 8, CADS) * keep[None]
    turned = pltpu.roll(values, 4, 1)
    upper = lax.broadcasted_iota(jnp.int32, (16, 8, CADS), 1) < 4
    zero = jnp.zeros_like(values)
    expanded[:, 0, :, :CADS] = jnp.where(upper, values, zero)
    expanded[:, 1, :, :CADS] = jnp.where(upper, turned, zero)
    expanded[:, 0, :, CADS:] = jnp.where(upper, zero, turned)
    expanded[:, 1, :, CADS:] = jnp.where(upper, zero, values)
    high, low = split(expanded[...].reshape(256, 2 * CADS))
    wide_high[...] = high
    wide_low[...] = low
    acc[...] = jnp.zeros_like(acc)
    logs[...] = jnp.zeros_like(logs)

    going = True
    while going:
        going = False
        for g in gathers:
            try:
                next(g)
                going = True
            except StopIteration:
                pass
    light_copy.wait()

    def block(j, carry):
        columns = pl.ds(pl.multiple_of(j * BLOCK, BLOCK), BLOCK)
        loads = slabs[:, :, :, columns].reshape(256, BLOCK)
        wide = (wide_high[...], wide_low[...])
        predicted = dot3(split(loads.T), wide, ((1,), (0,)))
        keep = good[...].astype(F32)
        weighted = []
        for half in range(2):
            rows = pl.ds(pl.multiple_of(half * HALF + j * BLOCK, BLOCK), BLOCK)
            side = slice(half * CADS, (half + 1) * CADS)
            residual = light[rows, :] * keep - predicted[:, side]
            ratio = 1.0 + (residual * 0.5) ** 2
            weighted.append(residual / ratio)
            four = ratio.reshape(4, BLOCK // 4, CADS)
            four = (four[0] * four[1]) * (four[2] * four[3])
            logs[:, side] += jnp.sum(jnp.log(four).reshape(BLOCK // 32, 8, CADS), axis=0)
        weighted = split(jnp.concatenate(weighted, axis=1))
        grads[:, :, :, columns] = dot3(wide, weighted, ((1,), (1,))).reshape(NZ, NX, 8, BLOCK)
        acc[...] += dot3(split(loads), weighted, ((1,), (0,))).reshape(acc.shape)
        return carry

    lax.fori_loop(0, HALF // BLOCK, block, 0)

    reduces = [reduce_rounds(i, *chunk, boxes[2 * i], boxes[2 * i + 1]) for i, chunk in enumerate(CHUNKS)]
    for g in reduces:
        next(g)

    top = lax.broadcasted_iota(jnp.int32, (16, 8, CADS), 1) < 4
    first, second = acc[:, 0, :, :], acc[:, 1, :, :]
    sums = jnp.where(
        top,
        first[:, :, :CADS] + pltpu.roll(first[:, :, CADS:], 4, 1),
        pltpu.roll(second[:, :, :CADS], 4, 1) + second[:, :, CADS:],
    )
    cad_part[:, :, 0:8, :] = sums.reshape(NY, 2, 8, CADS)
    log_sum = (logs[:, :CADS] + logs[:, CADS:])
    cad_part[:, :, 8:16, :] = jnp.broadcast_to(log_sum[None, None], (NY, 2, 8, CADS))
    across = remote(cad_part.at[:, 1 - core], cad_core, small_send.at[8], small_recv.at[8], partner)
    sent.append(across)
    for g in reduces:
        next(g)
    across.wait_recv()
    cad_part[:, core] = cad_part[:, core] + cad_core[...]
    arrivals = [
        remote(cad_part.at[at_y(d), core], cad_from.at[y], small_send.at[8 + d], small_recv.at[8 + d], to_y(d))
        for d in range(1, NY)
    ]
    sent.extend(arrivals)
    for g in reduces:
        next(g)
    cad_from[y] = cad_part[y, core]
    for copy in arrivals:
        copy.wait_recv()
    total = jnp.sum(cad_from[...], axis=0)
    cad_out[...] = total[0:8] * cad_scale
    loss_x[x] = total[8:16]
    loss_hops = [
        remote(loss_x.at[x], loss_x.at[x], small_send.at[15 + d], small_recv.at[15 + d], to_x(d))
        for d in range(1, NX)
    ]
    sent.extend(loss_hops)
    for g in reduces:
        next(g)
    for copy in loss_hops:
        copy.wait_recv()
    loss_z[z] = jnp.sum(loss_x[...], axis=0)
    loss_hops = [
        remote(loss_z.at[z], loss_z.at[z], small_send.at[18 + d], small_recv.at[18 + d], to_z(d))
        for d in range(1, NZ)
    ]
    sent.extend(loss_hops)
    for g in reduces:
        next(g)
    going = True
    while going:
        going = False
        for g in reduces:
            try:
                next(g)
                going = True
            except StopIteration:
                pass
    for copy in loss_hops:
        copy.wait_recv()
    everything = jnp.sum(loss_z[...], axis=0)
    loss_out[...] = jnp.sum(jnp.sum(everything, axis=0, keepdims=True), axis=1, keepdims=True) * loss_scale
    star_out[:, :HALF] = slabs_out(grads, z, x, 0) * star_scale
    star_out[:, HALF:] = slabs_out(grads, z, x, 4) * star_scale
    for copy in sent:
        copy.wait_send()


def slabs_out(grads, z, x, row):
    return grads[z, x, row:row + 4, :]


def on_device(light, quality, star_factors, cadence_factors):
    stars = light.shape[0] * lax.axis_size("star")
    cads = light.shape[1] * lax.axis_size("cad")
    dma = pltpu.SemaphoreType.DMA
    boxes = []
    for order, _, width in CHUNKS:
        far, near = ((NX, NZ) if order == "xz" else (NZ, NX))
        hops = {NX: 3, NZ: 7}
        boxes.append(pltpu.VMEM((hops[near], far, 8, width), F32))
        boxes.append(pltpu.VMEM((hops[far], 8, width), F32))
    count = len(CHUNKS) * MESSAGES
    any_space = pl.BlockSpec(memory_space=pl.ANY)
    vmem = pl.BlockSpec(memory_space=pltpu.VMEM)
    star_gradient, cadence_gradient, loss = pl.pallas_call(
        functools.partial(
            kernel, -1.0 / float(cads) ** 0.5, -1.0 / float(stars) ** 0.5, 2.0 / (float(stars) * float(cads))
        ),
        out_shape=(
            jax.ShapeDtypeStruct((4, 4096), F32),
            jax.ShapeDtypeStruct((8, CADS), F32),
            jax.ShapeDtypeStruct((1, 1), F32),
        ),
        in_specs=[any_space] * 4,
        out_specs=(vmem, vmem, vmem),
        scratch_shapes=[
            pltpu.VMEM((4096, CADS), F32),
            pltpu.VMEM((4, 4096), F32),
            pltpu.VMEM((NZ, NX, 8, HALF), F32),
            pltpu.VMEM((NZ, NX, 8, HALF), F32),
            pltpu.VMEM((NY, 2, 8, CADS), F32),
            pltpu.VMEM((16, 2, 8, 2 * CADS), F32),
            pltpu.VMEM((256, 2 * CADS), BF16),
            pltpu.VMEM((256, 2 * CADS), BF16),
            pltpu.VMEM((1, CADS), jnp.int32),
            pltpu.VMEM((16, 2, 8, 2 * CADS), F32),
            pltpu.VMEM((8, 2 * CADS), F32),
            pltpu.VMEM((NY, 2, 16, CADS), F32),
            pltpu.VMEM((NY, 16, CADS), F32),
            pltpu.VMEM((NY, 16, CADS), F32),
            pltpu.VMEM((NX, 8, CADS), F32),
            pltpu.VMEM((NZ, 8, CADS), F32),
            *boxes,
            dma((4,)),
            dma((count,)), dma((count,)), dma((count,)), dma((count,)), dma((26,)), dma((26,)),
        ],
        compiler_params=pltpu.CompilerParams(
            collective_id=0, has_side_effects=True, vmem_limit_bytes=60 << 20
        ),
        cost_estimate=pl.CostEstimate(flops=10**9, bytes_accessed=5 * 10**6, transcendentals=2 * 10**6),
        name="cauchy_factor_gradient",
    )(light, quality.reshape(1, CADS), star_factors.T, cadence_factors.T)
    return (star_gradient.T, cadence_gradient.T, loss.reshape(()))


def solution(mesh):
    in_specs = (P("star", "cad"), P("cad"), P("star", "cad"), P("cad", "star"))
    out_specs = (P("star", "cad"), P("cad", "star"), P())
    return jax.shard_map(
        on_device, mesh=mesh, in_specs=in_specs, out_specs=out_specs, check_vma=False
    )
```

```python
import functools

import jax
import jax.numpy as jnp
from jax import lax
from jax.experimental import pallas as pl
from jax.experimental.pallas import tpu as pltpu
from jax.sharding import PartitionSpec as P

MESH = pl.DeviceIdType.MESH
F32, BF16 = jnp.float32, jnp.bfloat16
NZ, NX, NY = 8, 4, 8
HALF = 2048
CADS = 256
BLOCK = 256
EDGES = NZ * NX - 1
STEP_Z = (
    (0, 0, 0, 0),
    (1, 0, 0, 0),
    (1, 1, 1, 0),
    (2, 0, 0, 0),
    (1, 1, -2, 0),
    (-1, -1, 0, 0),
    (-1, -2, 0, 0),
    (-1, 0, -1, 0),
)
STEP_X = (
    (0, 1, -1, -1),
    (0, 1, 1, -1),
    (0, 0, 0, -1),
    (0, 1, 1, -1),
    (0, 0, 0, -1),
    (0, 0, 1, -1),
    (0, 0, 1, -1),
    (0, 1, 0, -1),
)


def tree():
    parents = {
        (dz, dx): ((dz - STEP_Z[dz][dx]) % NZ, (dx - STEP_X[dz][dx]) % NX)
        for dz in range(NZ)
        for dx in range(NX)
        if dz or dx
    }

    def depth(place):
        return 1 + depth(parents[place]) if place in parents else 0

    levels = [[] for _ in range(max(map(depth, parents)))]
    for place, parent in parents.items():
        levels[depth(place) - 1].append((place, parent))
    return levels


TREE = tree()
LEVELS = len(TREE)
CHUNKS = ((0, 256), (256, 768), (1024, 512), (1536, 512))


def split(value):
    high = value.astype(BF16)
    return high, (value - high.astype(F32)).astype(BF16)


def dot3(a, b, dims):
    def one(p, q):
        return lax.dot_general(p, q, (dims, ((), ())), preferred_element_type=F32)

    return one(a[0], b[0]) + (one(a[0], b[1]) + one(a[1], b[0]))


def kernel(
    star_scale, cad_scale, loss_scale,
    light_ref, quality_ref, star_ref, cad_ref,
    star_out, cad_out, loss_out,
    light, own, slabs, grads, cads, expanded, wide_high, wide_low, good, acc, logs,
    cad_part, cad_core, cad_from, loss_x, loss_z, *rest,
):
    boxes, (sems, gather_send, gather_recv, reduce_send, reduce_recv, small_send, small_recv) = rest[:-7], rest[-7:]
    star, cad = lax.axis_index("star"), lax.axis_index("cad")
    y, core = star // 2, lax.rem(star, 2)
    z, x = cad // NX, lax.rem(cad, NX)

    def at_z(d):
        return lax.rem(z + d + NZ, NZ)

    def at_x(d):
        return lax.rem(x + d + NX, NX)

    def at_y(d):
        return lax.rem(y + d, NY)

    def to_z(d):
        return (star, at_z(d) * NX + x)

    def to_x(d):
        return (star, z * NX + at_x(d))

    def to_y(d):
        return (at_y(d) * 2 + core, cad)

    partner = (y * 2 + 1 - core, cad)

    light_copy = pltpu.make_async_copy(light_ref, light, sems.at[0])
    own_copy = pltpu.make_async_copy(star_ref, own, sems.at[1])
    cad_copy = pltpu.make_async_copy(cad_ref, cads.at[y, core], sems.at[2])
    good_copy = pltpu.make_async_copy(quality_ref, good, sems.at[3])
    own_copy.start()
    cad_copy.start()
    good_copy.start()

    barrier = pltpu.get_barrier_semaphore()
    peers = [to_z(d) for d in range(1, NZ)] + [to_x(d) for d in range(1, NX)]
    peers += [to_y(d) for d in range(1, NY)] + [partner]
    for peer in peers:
        pl.semaphore_signal(barrier, inc=1, device_id=peer, device_id_type=MESH)
    own_copy.wait()
    slabs[z, x, 0:4, :] = own[:, :HALF]
    slabs[z, x, 4:8, :] = own[:, HALF:]
    pl.semaphore_wait(barrier, len(peers))

    def remote(src, dst, send, recv, where):
        copy = pltpu.make_async_remote_copy(
            src_ref=src, dst_ref=dst, send_sem=send, recv_sem=recv,
            device_id=where, device_id_type=MESH,
        )
        copy.start()
        return copy

    sent = []

    def whole(offset):
        return (at_z(offset[0]), at_x(offset[1]))

    def minus(a, b=(0, 0)):
        return (b[0] - a[0], b[1] - a[1])

    def device(offset):
        places = whole(offset)
        return (star, places[0] * NX + places[1])

    def wait_for(ref, semaphore):
        pltpu.make_async_copy(ref, ref, semaphore).wait()

    def gather_rounds(index, first, width):
        columns = pl.ds(first, width)
        for level, edges in enumerate(TREE):
            if level:
                wait_for(boxes[index].at[:len(TREE[level - 1])], gather_recv.at[index, level - 1])
            for offset, parent in edges:
                slab = slabs.at[whole(minus(parent))].at[:, columns]
                remote(
                    slab, slab, gather_send.at[index], gather_recv.at[index, level], device(minus(parent, offset))
                )
            yield False
        wait_for(boxes[index].at[:len(TREE[-1])], gather_recv.at[index, LEVELS - 1])

    def reduce_rounds(index, first, width):
        columns = pl.ds(first, width)
        box = boxes[index]
        starts = [sum(len(edges) for edges in TREE[:level]) for level in range(LEVELS)]

        def gathered(offset, level):
            mine = grads.at[whole(minus(offset))].at[:, columns]
            total = None
            for n, (_, parent) in enumerate(TREE[level] if level < LEVELS else ()):
                if parent == offset:
                    n += starts[level]
                    total = box[n] if total is None else total + box[n]
            if total is not None:
                mine[...] = mine[...] + total
            return mine

        def landed(level):
            if level < LEVELS:
                wait_for(box.at[pl.ds(starts[level], len(TREE[level]))], reduce_recv.at[index, level])

        for level in reversed(range(LEVELS)):
            landed(level + 1)
            for n, (offset, parent) in enumerate(TREE[level]):
                remote(
                    gathered(offset, level + 1), box.at[starts[level] + n], reduce_send.at[index],
                    reduce_recv.at[index, level], device(minus(offset, parent)),
                )
            yield False
        landed(0)
        gathered((0, 0), 0)

    cad_copy.wait()
    cad_in = [
        remote(cads.at[y, core], cads.at[y, core], small_send.at[d - 1], small_recv.at[d - 1], to_y(d))
        for d in range(1, NY)
    ]
    sent.extend(cad_in)
    gathers = [gather_rounds(i, *chunk) for i, chunk in enumerate(CHUNKS)]
    reduces = [reduce_rounds(i, *chunk) for i, chunk in enumerate(CHUNKS)]
    begun = []

    def advance(rounds):
        for g in tuple(rounds):
            if next(g, True):
                rounds.remove(g)

    advance(list(gathers))
    light_copy.start()
    ahead, others = gathers[:1], gathers[1:]
    advance(list(ahead))
    advance(list(others))
    advance(list(ahead))
    for copy in cad_in:
        copy.wait_recv()
    cad_across = remote(cads.at[:, core], cads.at[:, core], small_send.at[7], small_recv.at[7], partner)
    sent.append(cad_across)
    advance(list(others))
    advance(list(ahead))
    cad_across.wait_recv()

    good_copy.wait()
    keep = good[...].astype(F32)
    values = cads[...].reshape(16, 8, CADS) * keep[None]
    turned = pltpu.roll(values, 4, 1)
    upper = lax.broadcasted_iota(jnp.int32, (16, 8, CADS), 1) < 4
    zero = jnp.zeros_like(values)
    expanded[:, 0, :, :CADS] = jnp.where(upper, values, zero)
    expanded[:, 1, :, :CADS] = jnp.where(upper, turned, zero)
    expanded[:, 0, :, CADS:] = jnp.where(upper, zero, turned)
    expanded[:, 1, :, CADS:] = jnp.where(upper, zero, values)
    high, low = split(expanded[...].reshape(256, 2 * CADS))
    wide_high[...] = high
    wide_low[...] = low
    acc[...] = jnp.zeros_like(acc)
    logs[...] = jnp.zeros_like(logs)

    for _ in range(3, LEVELS):
        advance(list(others))
        advance(list(ahead))
    light_copy.wait()

    def block(j, carry):
        columns = pl.ds(pl.multiple_of(j * BLOCK, BLOCK), BLOCK)
        loads = slabs[:, :, :, columns].reshape(256, BLOCK)
        wide = (wide_high[...], wide_low[...])
        predicted = dot3(split(loads.T), wide, ((1,), (0,)))
        keep = good[...].astype(F32)
        weighted = []
        for half in range(2):
            rows = pl.ds(pl.multiple_of(half * HALF + j * BLOCK, BLOCK), BLOCK)
            side = slice(half * CADS, (half + 1) * CADS)
            residual = light[rows, :] * keep - predicted[:, side]
            ratio = 1.0 + (residual * 0.5) ** 2
            weighted.append(residual / ratio)
            four = ratio.reshape(4, BLOCK // 4, CADS)
            four = (four[0] * four[1]) * (four[2] * four[3])
            logs[:, side] += jnp.sum(jnp.log(four).reshape(BLOCK // 32, 8, CADS), axis=0)
        weighted = split(jnp.concatenate(weighted, axis=1))
        grads[:, :, :, columns] = dot3(wide, weighted, ((1,), (1,))).reshape(NZ, NX, 8, BLOCK)
        acc[...] += dot3(split(loads), weighted, ((1,), (0,))).reshape(acc.shape)
        return carry

    for i, (first, width) in enumerate(CHUNKS):
        next(gathers[i], None)
        lax.fori_loop(first // BLOCK, (first + width) // BLOCK, block, 0)
        begun.append(reduces[i])
        advance(begun)

    top = lax.broadcasted_iota(jnp.int32, (16, 8, CADS), 1) < 4
    first, second = acc[:, 0, :, :], acc[:, 1, :, :]
    sums = jnp.where(
        top,
        first[:, :, :CADS] + pltpu.roll(first[:, :, CADS:], 4, 1),
        pltpu.roll(second[:, :, :CADS], 4, 1) + second[:, :, CADS:],
    )
    cad_part[:, :, 0:8, :] = sums.reshape(NY, 2, 8, CADS)
    log_sum = (logs[:, :CADS] + logs[:, CADS:])
    cad_part[:, :, 8:16, :] = jnp.broadcast_to(log_sum[None, None], (NY, 2, 8, CADS))
    across = remote(cad_part.at[:, 1 - core], cad_core, small_send.at[8], small_recv.at[8], partner)
    sent.append(across)
    across.wait_recv()
    cad_part[:, core] = cad_part[:, core] + cad_core[...]
    arrivals = [
        remote(cad_part.at[at_y(d), core], cad_from.at[y], small_send.at[8 + d], small_recv.at[8 + d], to_y(d))
        for d in range(1, NY)
    ]
    sent.extend(arrivals)
    cad_from[y] = cad_part[y, core]
    advance(begun)
    for i in range(len(CHUNKS)):
        wait_for(boxes[i], gather_send.at[i])
    advance(begun)
    for copy in arrivals:
        copy.wait_recv()
    total = jnp.sum(cad_from[...], axis=0)
    loss_x[x] = total[8:16]
    loss_hops = [
        remote(loss_x.at[x], loss_x.at[x], small_send.at[15 + d], small_recv.at[15 + d], to_x(d))
        for d in range(1, NX)
    ]
    sent.extend(loss_hops)
    cad_out[...] = total[0:8] * cad_scale
    advance(begun)
    for copy in loss_hops:
        copy.wait_recv()
    loss_z[z] = jnp.sum(loss_x[...], axis=0)
    loss_hops = [
        remote(loss_z.at[z], loss_z.at[z], small_send.at[18 + d], small_recv.at[18 + d], to_z(d))
        for d in range(1, NZ)
    ]
    advance(begun)
    for copy in sent:
        copy.wait_send()
    advance(begun)
    for copy in loss_hops:
        copy.wait_recv()
    everything = jnp.sum(loss_z[...], axis=0)
    loss_out[...] = jnp.sum(jnp.sum(everything, axis=0, keepdims=True), axis=1, keepdims=True) * loss_scale
    for copy in loss_hops:
        copy.wait_send()
    while begun:
        advance(begun)
    for i in range(len(CHUNKS)):
        wait_for(boxes[i], reduce_send.at[i])
    star_out[:, :HALF] = grads[z, x, 0:4, :] * star_scale
    star_out[:, HALF:] = grads[z, x, 4:8, :] * star_scale


def on_device(light, quality, star_factors, cadence_factors):
    stars = light.shape[0] * lax.axis_size("star")
    cads = light.shape[1] * lax.axis_size("cad")
    dma = pltpu.SemaphoreType.DMA
    boxes = [pltpu.VMEM((EDGES, 8, width), F32) for _, width in CHUNKS]
    count = len(CHUNKS)
    hbm = pl.BlockSpec(memory_space=pltpu.HBM)
    vmem = pl.BlockSpec(memory_space=pltpu.VMEM)
    star_gradient, cadence_gradient, loss = pl.pallas_call(
        functools.partial(
            kernel, -1.0 / float(cads) ** 0.5, -1.0 / float(stars) ** 0.5, 2.0 / (float(stars) * float(cads))
        ),
        out_shape=(
            jax.ShapeDtypeStruct((4, 4096), F32),
            jax.ShapeDtypeStruct((8, CADS), F32),
            jax.ShapeDtypeStruct((1, 1), F32),
        ),
        in_specs=[hbm] * 4,
        out_specs=(vmem, vmem, vmem),
        scratch_shapes=[
            pltpu.VMEM((4096, CADS), F32),
            pltpu.VMEM((4, 4096), F32),
            pltpu.VMEM((NZ, NX, 8, HALF), F32),
            pltpu.VMEM((NZ, NX, 8, HALF), F32),
            pltpu.VMEM((NY, 2, 8, CADS), F32),
            pltpu.VMEM((16, 2, 8, 2 * CADS), F32),
            pltpu.VMEM((256, 2 * CADS), BF16),
            pltpu.VMEM((256, 2 * CADS), BF16),
            pltpu.VMEM((1, CADS), jnp.int32),
            pltpu.VMEM((16, 2, 8, 2 * CADS), F32),
            pltpu.VMEM((8, 2 * CADS), F32),
            pltpu.VMEM((NY, 2, 16, CADS), F32),
            pltpu.VMEM((NY, 16, CADS), F32),
            pltpu.VMEM((NY, 16, CADS), F32),
            pltpu.VMEM((NX, 8, CADS), F32),
            pltpu.VMEM((NZ, 8, CADS), F32),
            *boxes,
            dma((4,)),
            dma((count,)), dma((count, LEVELS)), dma((count,)), dma((count, LEVELS)), dma((26,)), dma((26,)),
        ],
        compiler_params=pltpu.CompilerParams(
            collective_id=0, has_side_effects=True, vmem_limit_bytes=40 << 20
        ),
        cost_estimate=pl.CostEstimate(flops=10**9, bytes_accessed=5 * 10**6, transcendentals=2 * 10**6),
        name="cauchy_factor_gradient",
    )(*(
        pltpu.with_memory_space_constraint(array, pltpu.HBM)
        for array in (light, quality.reshape(1, CADS), star_factors.T, cadence_factors.T)
    ))
    return (star_gradient.T, cadence_gradient.T, loss.reshape(()))


def solution(mesh):
    in_specs = (P("star", "cad"), P("cad"), P("star", "cad"), P("cad", "star"))
    out_specs = (P("star", "cad"), P("cad", "star"), P())
    return jax.shard_map(
        on_device, mesh=mesh, in_specs=in_specs, out_specs=out_specs, check_vma=False
    )
```

```python
import functools

import jax
import jax.numpy as jnp
from jax import lax
from jax.experimental import pallas as pl
from jax.experimental.pallas import tpu as pltpu
from jax.sharding import PartitionSpec as P

MESH = pl.DeviceIdType.MESH
F32, BF16 = jnp.float32, jnp.bfloat16
NZ, NX, NY = 8, 4, 8
HALF = 2048
CADS = 256
BLOCK = 256
EDGES = NZ * NX - 1
STEP_Z = (
    (0, 0, 0, 0),
    (1, 0, 0, 0),
    (1, 1, 1, 0),
    (2, 0, 0, 0),
    (1, 1, -2, 0),
    (-1, -1, 0, 0),
    (-1, -2, 0, 0),
    (-1, 0, -1, 0),
)
STEP_X = (
    (0, 1, -1, -1),
    (0, 1, 1, -1),
    (0, 0, 0, -1),
    (0, 1, 1, -1),
    (0, 0, 0, -1),
    (0, 0, 1, -1),
    (0, 0, 1, -1),
    (0, 1, 0, -1),
)


def tree():
    parents = {
        (dz, dx): ((dz - STEP_Z[dz][dx]) % NZ, (dx - STEP_X[dz][dx]) % NX)
        for dz in range(NZ)
        for dx in range(NX)
        if dz or dx
    }

    def depth(place):
        return 1 + depth(parents[place]) if place in parents else 0

    levels = [[] for _ in range(max(map(depth, parents)))]
    for place, parent in parents.items():
        levels[depth(place) - 1].append((place, parent))
    return levels


TREE = tree()
LEVELS = len(TREE)
CHUNKS = ((0, 512), (512, 512), (1024, 512), (1536, 512))


def split(value):
    high = value.astype(BF16)
    return high, (value - high.astype(F32)).astype(BF16)


def dot3(a, b, dims):
    def one(p, q):
        return lax.dot_general(p, q, (dims, ((), ())), preferred_element_type=F32)

    rows = a[0].shape[0]
    both = one(jnp.concatenate(a, axis=0), b[0])
    return both[:rows] + (one(a[0], b[1]) + both[rows:])


def kernel(
    star_scale, cad_scale, loss_scale,
    light_ref, quality_ref, star_ref, cad_ref,
    star_out, cad_out, loss_out,
    light, own, slabs, grads, cads, expanded, wide_high, wide_low, good, acc, logs,
    cad_part, cad_core, cad_from, loss_core, loss_y, loss_x, loss_z, *rest,
):
    boxes, (sems, gather_send, gather_recv, reduce_send, reduce_recv, small_send, small_recv) = rest[:-7], rest[-7:]
    star, cad = lax.axis_index("star"), lax.axis_index("cad")
    y, core = star // 2, lax.rem(star, 2)
    z, x = cad // NX, lax.rem(cad, NX)

    def at_z(d):
        return lax.rem(z + d + NZ, NZ)

    def at_x(d):
        return lax.rem(x + d + NX, NX)

    def at_y(d):
        return lax.rem(y + d, NY)

    def to_z(d):
        return (star, at_z(d) * NX + x)

    def to_x(d):
        return (star, z * NX + at_x(d))

    def to_y(d):
        return (at_y(d) * 2 + core, cad)

    partner = (y * 2 + 1 - core, cad)

    light_copy = pltpu.make_async_copy(light_ref, light, sems.at[0])
    own_copy = pltpu.make_async_copy(star_ref, own, sems.at[1])
    cad_copy = pltpu.make_async_copy(cad_ref, cads.at[y, core], sems.at[2])
    good_copy = pltpu.make_async_copy(quality_ref, good, sems.at[3])
    own_copy.start()
    cad_copy.start()
    good_copy.start()

    barrier = pltpu.get_barrier_semaphore()
    peers = [to_z(d) for d in range(1, NZ)] + [to_x(d) for d in range(1, NX)]
    peers += [to_y(d) for d in range(1, NY)] + [partner]
    for peer in peers:
        pl.semaphore_signal(barrier, inc=1, device_id=peer, device_id_type=MESH)
    own_copy.wait()
    slabs[z, x, 0:4, :] = own[:, :HALF]
    slabs[z, x, 4:8, :] = own[:, HALF:]
    pl.semaphore_wait(barrier, len(peers))

    def remote(src, dst, send, recv, where):
        copy = pltpu.make_async_remote_copy(
            src_ref=src, dst_ref=dst, send_sem=send, recv_sem=recv,
            device_id=where, device_id_type=MESH,
        )
        copy.start()
        return copy

    sent = []

    def whole(offset):
        return (at_z(offset[0]), at_x(offset[1]))

    def minus(a, b=(0, 0)):
        return (b[0] - a[0], b[1] - a[1])

    def device(offset):
        places = whole(offset)
        return (star, places[0] * NX + places[1])

    def wait_for(ref, semaphore):
        pltpu.make_async_copy(ref, ref, semaphore).wait()

    def gather_rounds(index, first, width):
        columns = pl.ds(first, width)
        for level, edges in enumerate(TREE):
            if level:
                wait_for(boxes[index].at[:len(TREE[level - 1])], gather_recv.at[index, level - 1])
            for offset, parent in edges:
                slab = slabs.at[whole(minus(parent))].at[:, columns]
                remote(
                    slab, slab, gather_send.at[index], gather_recv.at[index, level], device(minus(parent, offset))
                )
            yield False
        wait_for(boxes[index].at[:len(TREE[-1])], gather_recv.at[index, LEVELS - 1])

    def reduce_rounds(index, first, width):
        columns = pl.ds(first, width)
        box = boxes[index]
        starts = [sum(len(edges) for edges in TREE[:level]) for level in range(LEVELS)]

        def gathered(offset, level):
            mine = grads.at[whole(minus(offset))].at[:, columns]
            total = None
            for n, (_, parent) in enumerate(TREE[level] if level < LEVELS else ()):
                if parent == offset:
                    n += starts[level]
                    total = box[n] if total is None else total + box[n]
            if total is not None:
                mine[...] = mine[...] + total
            return mine

        def landed(level):
            if level < LEVELS:
                wait_for(box.at[pl.ds(starts[level], len(TREE[level]))], reduce_recv.at[index, level])

        for level in reversed(range(LEVELS)):
            landed(level + 1)
            for n, (offset, parent) in enumerate(TREE[level]):
                remote(
                    gathered(offset, level + 1), box.at[starts[level] + n], reduce_send.at[index],
                    reduce_recv.at[index, level], device(minus(offset, parent)),
                )
            yield False
        landed(0)
        gathered((0, 0), 0)

    cad_copy.wait()
    cad_in = [
        remote(cads.at[y, core], cads.at[y, core], small_send.at[d - 1], small_recv.at[d - 1], to_y(d))
        for d in range(1, NY)
    ]
    sent.extend(cad_in)
    gathers = [gather_rounds(i, *chunk) for i, chunk in enumerate(CHUNKS)]
    reduces = [reduce_rounds(i, *chunk) for i, chunk in enumerate(CHUNKS)]

    def advance(rounds):
        for g in tuple(rounds):
            if next(g, True):
                rounds.remove(g)

    advance(list(gathers))
    light_copy.start()
    ahead, others = gathers[:1], gathers[1:]
    advance(list(ahead))
    advance(list(others))
    advance(list(ahead))
    for copy in cad_in:
        copy.wait_recv()
    cad_across = remote(cads.at[:, core], cads.at[:, core], small_send.at[7], small_recv.at[7], partner)
    sent.append(cad_across)
    advance(list(others))
    advance(list(ahead))
    cad_across.wait_recv()

    good_copy.wait()
    keep = good[...].astype(F32)
    values = cads[...].reshape(16, 8, CADS) * keep[None]
    turned = pltpu.roll(values, 4, 1)
    upper = lax.broadcasted_iota(jnp.int32, (16, 8, CADS), 1) < 4
    zero = jnp.zeros_like(values)
    expanded[:, 0, :, :CADS] = jnp.where(upper, values, zero)
    expanded[:, 1, :, :CADS] = jnp.where(upper, turned, zero)
    expanded[:, 0, :, CADS:] = jnp.where(upper, zero, turned)
    expanded[:, 1, :, CADS:] = jnp.where(upper, zero, values)
    high, low = split(expanded[...].reshape(256, 2 * CADS))
    wide_high[...] = high
    wide_low[...] = low
    acc[...] = jnp.zeros_like(acc)
    logs[...] = jnp.zeros_like(logs)

    for _ in range(3, LEVELS):
        advance(list(others))
        advance(list(ahead))
    light_copy.wait()

    def block(j, carry):
        columns = pl.ds(pl.multiple_of(j * BLOCK, BLOCK), BLOCK)
        loads = slabs[:, :, :, columns].reshape(256, BLOCK)
        wide = (wide_high[...], wide_low[...])
        predicted = dot3(split(loads.T), wide, ((1,), (0,)))
        keep = good[...].astype(F32)
        weighted = []
        for half in range(2):
            rows = pl.ds(pl.multiple_of(half * HALF + j * BLOCK, BLOCK), BLOCK)
            side = slice(half * CADS, (half + 1) * CADS)
            residual = light[rows, :] * keep - predicted[:, side]
            ratio = 1.0 + (residual * 0.5) ** 2
            weighted.append(residual * pl.reciprocal(ratio))
            four = ratio.reshape(4, BLOCK // 4, CADS)
            four = (four[0] * four[1]) * (four[2] * four[3])
            logs[:, side] += jnp.sum(jnp.log(four).reshape(BLOCK // 32, 8, CADS), axis=0)
        weighted = split(jnp.concatenate(weighted, axis=1))
        grads[:, :, :, columns] = dot3(wide, weighted, ((1,), (1,))).reshape(NZ, NX, 8, BLOCK)
        acc[...] += dot3(split(loads), weighted, ((1,), (0,))).reshape(acc.shape)
        return carry

    def step(*which):
        for i in which:
            next(reduces[i], None)

    for i, (first, width) in enumerate(CHUNKS):
        next(gathers[i], None)
        lax.fori_loop(first // BLOCK, (first + width) // BLOCK, block, 0, unroll=True)
        step(*range(i, -1, -2))

    log_sum = (logs[:, :128] + logs[:, 128:256]) + (logs[:, 256:384] + logs[:, 384:])
    loss_core[core] = log_sum
    loss_hop = remote(loss_core.at[core], loss_core.at[core], small_send.at[25], small_recv.at[25], partner)
    sent.append(loss_hop)

    top = lax.broadcasted_iota(jnp.int32, (16, 8, CADS), 1) < 4
    first, second = acc[:, 0, :, :], acc[:, 1, :, :]
    sums = jnp.where(
        top,
        first[:, :, :CADS] + pltpu.roll(first[:, :, CADS:], 4, 1),
        pltpu.roll(second[:, :, :CADS], 4, 1) + second[:, :, CADS:],
    )
    cad_part[...] = sums.reshape(NY, 2, 8, CADS)
    across = remote(cad_part.at[:, 1 - core], cad_core, small_send.at[8], small_recv.at[8], partner)
    sent.append(across)

    def exchange(ref, place, first, peers):
        copies = [
            remote(ref.at[place], ref.at[place], small_send.at[first + n], small_recv.at[first + n], peer)
            for n, peer in enumerate(peers)
        ]
        sent.extend(copies)
        return copies

    def arrive(copies):
        for copy in copies:
            copy.wait_recv()

    last = len(CHUNKS) - 1
    older = tuple(range(last - 1, -1, -1))
    loss_hop.wait_recv()
    loss_y[y] = loss_core[0] + loss_core[1]
    loss_hops = exchange(loss_y, y, 26, [to_y(d) for d in range(1, NY)])
    across.wait_recv()
    cad_part[:, core] = cad_part[:, core] + cad_core[...]
    cad_from[y] = cad_part[y, core]
    arrivals = [
        remote(cad_part.at[at_y(d), core], cad_from.at[y], small_send.at[8 + d], small_recv.at[8 + d], to_y(d))
        for d in range(1, NY)
    ]
    sent.extend(arrivals)
    step(last - 1, last, *older)
    arrive(loss_hops)
    loss_x[x] = jnp.sum(loss_y[...], axis=0)
    loss_hops = exchange(loss_x, x, 16, [to_x(d) for d in range(1, NX)])
    step(last, *older)
    arrive(loss_hops)
    loss_z[z] = jnp.sum(loss_x[...], axis=0)
    loss_hops = exchange(loss_z, z, 19, [to_z(d) for d in range(1, NZ - 1)]) + exchange(loss_z, z, 33, [to_z(NZ - 1)])
    step(last, *older)
    arrive(arrivals)
    cad_out[...] = jnp.sum(cad_from[...], axis=0) * cad_scale
    for i in range(len(CHUNKS)):
        wait_for(boxes[i], gather_send.at[i])
    for copy in sent:
        copy.wait_send()
    arrive(loss_hops)
    everything = jnp.sum(loss_z[...], axis=0)
    loss_out[...] = jnp.sum(jnp.sum(everything, axis=0, keepdims=True), axis=1, keepdims=True) * loss_scale
    for _ in range(LEVELS):
        step(*range(len(CHUNKS)))
    for i in range(len(CHUNKS)):
        wait_for(boxes[i], reduce_send.at[i])
    star_out[:, :HALF] = grads[z, x, 0:4, :] * star_scale
    star_out[:, HALF:] = grads[z, x, 4:8, :] * star_scale


def on_device(light, quality, star_factors, cadence_factors):
    stars = light.shape[0] * lax.axis_size("star")
    cads = light.shape[1] * lax.axis_size("cad")
    dma = pltpu.SemaphoreType.DMA
    boxes = [pltpu.VMEM((EDGES, 8, width), F32) for _, width in CHUNKS]
    count = len(CHUNKS)
    hbm = pl.BlockSpec(memory_space=pltpu.HBM)
    vmem = pl.BlockSpec(memory_space=pltpu.VMEM)
    star_gradient, cadence_gradient, loss = pl.pallas_call(
        functools.partial(
            kernel, -1.0 / float(cads) ** 0.5, -1.0 / float(stars) ** 0.5, 2.0 / (float(stars) * float(cads))
        ),
        out_shape=(
            jax.ShapeDtypeStruct((4, 4096), F32),
            jax.ShapeDtypeStruct((8, CADS), F32),
            jax.ShapeDtypeStruct((1, 1), F32),
        ),
        in_specs=[hbm] * 4,
        out_specs=(vmem, vmem, vmem),
        scratch_shapes=[
            pltpu.VMEM((4096, CADS), F32),
            pltpu.VMEM((4, 4096), F32),
            pltpu.VMEM((NZ, NX, 8, HALF), F32),
            pltpu.VMEM((NZ, NX, 8, HALF), F32),
            pltpu.VMEM((NY, 2, 8, CADS), F32),
            pltpu.VMEM((16, 2, 8, 2 * CADS), F32),
            pltpu.VMEM((256, 2 * CADS), BF16),
            pltpu.VMEM((256, 2 * CADS), BF16),
            pltpu.VMEM((1, CADS), jnp.int32),
            pltpu.VMEM((16, 2, 8, 2 * CADS), F32),
            pltpu.VMEM((8, 2 * CADS), F32),
            pltpu.VMEM((NY, 2, 8, CADS), F32),
            pltpu.VMEM((NY, 8, CADS), F32),
            pltpu.VMEM((NY, 8, CADS), F32),
            pltpu.VMEM((2, 8, 128), F32),
            pltpu.VMEM((NY, 8, 128), F32),
            pltpu.VMEM((NX, 8, 128), F32),
            pltpu.VMEM((NZ, 8, 128), F32),
            *boxes,
            dma((4,)),
            dma((count,)), dma((count, LEVELS)), dma((count,)), dma((count, LEVELS)), dma((34,)), dma((34,)),
        ],
        compiler_params=pltpu.CompilerParams(
            collective_id=0, has_side_effects=True, vmem_limit_bytes=40 << 20
        ),
        cost_estimate=pl.CostEstimate(flops=10**9, bytes_accessed=5 * 10**6, transcendentals=2 * 10**6),
        name="cauchy_factor_gradient",
    )(*(
        pltpu.with_memory_space_constraint(array, pltpu.HBM)
        for array in (light, quality.reshape(1, CADS), star_factors.T, cadence_factors.T)
    ))
    return (star_gradient.T, cadence_gradient.T, loss.reshape(()))


def solution(mesh):
    in_specs = (P("star", "cad"), P("cad"), P("star", "cad"), P("cad", "star"))
    out_specs = (P("star", "cad"), P("cad", "star"), P())
    return jax.shard_map(
        on_device, mesh=mesh, in_specs=in_specs, out_specs=out_specs, check_vma=False
    )
```

```python
import functools

import jax
import jax.numpy as jnp
from jax import lax
from jax.experimental import pallas as pl
from jax.experimental.pallas import tpu as pltpu
from jax.sharding import PartitionSpec as P

MESH = pl.DeviceIdType.MESH
F32, BF16 = jnp.float32, jnp.bfloat16
NZ, NX, NY = 8, 4, 8
HALF = 2048
CADS = 256
BLOCK = 256
EDGES = NZ * NX - 1
STEP_Z = (
    (0, 0, 0, 0),
    (1, 0, 0, 0),
    (1, 1, 1, 0),
    (2, 0, 0, 0),
    (1, 1, -2, 0),
    (-1, -1, 0, 0),
    (-1, -2, 0, 0),
    (-1, 0, -1, 0),
)
STEP_X = (
    (0, 1, -1, -1),
    (0, 1, 1, -1),
    (0, 0, 0, -1),
    (0, 1, 1, -1),
    (0, 0, 0, -1),
    (0, 0, 1, -1),
    (0, 0, 1, -1),
    (0, 1, 0, -1),
)


def tree():
    parents = {
        (dz, dx): ((dz - STEP_Z[dz][dx]) % NZ, (dx - STEP_X[dz][dx]) % NX)
        for dz in range(NZ)
        for dx in range(NX)
        if dz or dx
    }

    def depth(place):
        return 1 + depth(parents[place]) if place in parents else 0

    levels = [[] for _ in range(max(map(depth, parents)))]
    for place, parent in parents.items():
        levels[depth(place) - 1].append((place, parent))
    return levels


TREE = tree()
LEVELS = len(TREE)
CHUNKS = ((0, 512), (512, 512), (1024, 512), (1536, 512))
AFTER = ((), (0,), (), (1,), (), (2, 0), (), (3, 1))
TAIL = ((0, 2), (3, 1, 2, 0), (3, 2, 1, 0), (3, 2, 1, 0))


def split(value):
    high = value.astype(BF16)
    return high, (value - high.astype(F32)).astype(BF16)


def dot3(a, b, dims):
    def one(p, q):
        return lax.dot_general(p, q, (dims, ((), ())), preferred_element_type=F32)

    rows = a[0].shape[0]
    both = one(jnp.concatenate(a, axis=0), b[0])
    return both[:rows] + (one(a[0], b[1]) + both[rows:])


def kernel(
    star_scale, cad_scale, loss_scale,
    light_ref, quality_ref, star_ref, cad_ref,
    star_out, cad_out, loss_out,
    light, own, slabs, grads, cads, expanded, wide_high, wide_low, good, acc, logs,
    cad_part, cad_core, cad_from, loss_core, loss_y, loss_x, loss_z, *rest,
):
    boxes, (sems, gather_send, gather_recv, reduce_send, reduce_recv, small_send, small_recv) = rest[:-7], rest[-7:]
    star, cad = lax.axis_index("star"), lax.axis_index("cad")
    y, core = star // 2, lax.rem(star, 2)
    z, x = cad // NX, lax.rem(cad, NX)

    def at_z(d):
        return lax.rem(z + d + NZ, NZ)

    def at_x(d):
        return lax.rem(x + d + NX, NX)

    def at_y(d):
        return lax.rem(y + d, NY)

    def to_z(d):
        return (star, at_z(d) * NX + x)

    def to_x(d):
        return (star, z * NX + at_x(d))

    def to_y(d):
        return (at_y(d) * 2 + core, cad)

    partner = (y * 2 + 1 - core, cad)

    light_copy = pltpu.make_async_copy(light_ref, light, sems.at[0])
    own_copy = pltpu.make_async_copy(star_ref, own, sems.at[1])
    cad_copy = pltpu.make_async_copy(cad_ref, cads.at[y, core], sems.at[2])
    good_copy = pltpu.make_async_copy(quality_ref, good, sems.at[3])
    own_copy.start()
    cad_copy.start()
    good_copy.start()

    barrier = pltpu.get_barrier_semaphore()
    peers = [to_z(d) for d in range(1, NZ)] + [to_x(d) for d in range(1, NX)]
    peers += [to_y(d) for d in range(1, NY)] + [partner]
    for peer in peers:
        pl.semaphore_signal(barrier, inc=1, device_id=peer, device_id_type=MESH)
    own_copy.wait()
    slabs[z, x, 0:4, :] = own[:, :HALF]
    slabs[z, x, 4:8, :] = own[:, HALF:]
    pl.semaphore_wait(barrier, len(peers))

    def remote(src, dst, send, recv, where):
        copy = pltpu.make_async_remote_copy(
            src_ref=src, dst_ref=dst, send_sem=send, recv_sem=recv,
            device_id=where, device_id_type=MESH,
        )
        copy.start()
        return copy

    sent = []

    def whole(offset):
        return (at_z(offset[0]), at_x(offset[1]))

    def minus(a, b=(0, 0)):
        return (b[0] - a[0], b[1] - a[1])

    def device(offset):
        places = whole(offset)
        return (star, places[0] * NX + places[1])

    def wait_for(ref, semaphore):
        pltpu.make_async_copy(ref, ref, semaphore).wait()

    def gather_rounds(index, first, width):
        columns = pl.ds(first, width)
        for level, edges in enumerate(TREE):
            if level:
                wait_for(boxes[index].at[:len(TREE[level - 1])], gather_recv.at[index, level - 1])
            for offset, parent in edges:
                slab = slabs.at[whole(minus(parent))].at[:, columns]
                remote(
                    slab, slab, gather_send.at[index], gather_recv.at[index, level], device(minus(parent, offset))
                )
            yield False
        wait_for(boxes[index].at[:len(TREE[-1])], gather_recv.at[index, LEVELS - 1])

    def reduce_rounds(index, first, width):
        columns = pl.ds(first, width)
        box = boxes[index]
        starts = [sum(len(edges) for edges in TREE[:level]) for level in range(LEVELS)]

        def gathered(offset, level):
            mine = grads.at[whole(minus(offset))].at[:, columns]
            total = None
            for n, (_, parent) in enumerate(TREE[level] if level < LEVELS else ()):
                if parent == offset:
                    n += starts[level]
                    total = box[n] if total is None else total + box[n]
            if total is not None:
                mine[...] = mine[...] + total
            return mine

        def landed(level):
            if level < LEVELS:
                wait_for(box.at[pl.ds(starts[level], len(TREE[level]))], reduce_recv.at[index, level])

        for level in reversed(range(LEVELS)):
            landed(level + 1)
            for n, (offset, parent) in enumerate(TREE[level]):
                remote(
                    gathered(offset, level + 1), box.at[starts[level] + n], reduce_send.at[index],
                    reduce_recv.at[index, level], device(minus(offset, parent)),
                )
            yield False
        landed(0)
        gathered((0, 0), 0)

    cad_copy.wait()
    cad_in = [
        remote(cads.at[y, core], cads.at[y, core], small_send.at[d - 1], small_recv.at[d - 1], to_y(d))
        for d in range(1, NY)
    ]
    sent.extend(cad_in)
    gathers = [gather_rounds(i, *chunk) for i, chunk in enumerate(CHUNKS)]
    reduces = [reduce_rounds(i, *chunk) for i, chunk in enumerate(CHUNKS)]

    def advance(rounds):
        for g in tuple(rounds):
            if next(g, True):
                rounds.remove(g)

    advance(list(gathers))
    light_copy.start()
    ahead, others = gathers[:1], gathers[1:]
    advance(list(ahead))
    advance(list(others))
    advance(list(ahead))
    for copy in cad_in:
        copy.wait_recv()
    cad_across = remote(cads.at[:, core], cads.at[:, core], small_send.at[7], small_recv.at[7], partner)
    sent.append(cad_across)
    advance(list(others))
    advance(list(ahead))
    cad_across.wait_recv()

    good_copy.wait()
    keep = good[...].astype(F32)
    values = cads[...].reshape(16, 8, CADS) * keep[None]
    turned = pltpu.roll(values, 4, 1)
    upper = lax.broadcasted_iota(jnp.int32, (16, 8, CADS), 1) < 4
    zero = jnp.zeros_like(values)
    expanded[:, 0, :, :CADS] = jnp.where(upper, values, zero)
    expanded[:, 1, :, :CADS] = jnp.where(upper, turned, zero)
    expanded[:, 0, :, CADS:] = jnp.where(upper, zero, turned)
    expanded[:, 1, :, CADS:] = jnp.where(upper, zero, values)
    high, low = split(expanded[...].reshape(256, 2 * CADS))
    wide_high[...] = high
    wide_low[...] = low
    acc[...] = jnp.zeros_like(acc)
    logs[...] = jnp.zeros_like(logs)

    for _ in range(3, LEVELS):
        advance(list(others))
        advance(list(ahead))
    light_copy.wait()

    def block(j):
        columns = pl.ds(j * BLOCK, BLOCK)
        loads = slabs[:, :, :, columns].reshape(256, BLOCK)
        wide = (wide_high[...], wide_low[...])
        predicted = dot3(split(loads.T), wide, ((1,), (0,)))
        keep = good[...].astype(F32)
        weighted = []
        for half in range(2):
            rows = pl.ds(half * HALF + j * BLOCK, BLOCK)
            side = slice(half * CADS, (half + 1) * CADS)
            residual = light[rows, :] * keep - predicted[:, side]
            ratio = 1.0 + (residual * 0.5) ** 2
            weighted.append(residual * pl.reciprocal(ratio))
            four = ratio.reshape(4, BLOCK // 4, CADS)
            four = (four[0] * four[1]) * (four[2] * four[3])
            logs[:, side] += jnp.sum(jnp.log(four).reshape(BLOCK // 32, 8, CADS), axis=0)
        weighted = split(jnp.concatenate(weighted, axis=1))
        grads[:, :, :, columns] = dot3(wide, weighted, ((1,), (1,))).reshape(NZ, NX, 8, BLOCK)
        acc[...] += dot3(split(loads), weighted, ((1,), (0,))).reshape(acc.shape)

    def step(*which):
        for i in which:
            next(reduces[i], None)

    for i, (first, width) in enumerate(CHUNKS):
        next(gathers[i], None)
        for j in range(first // BLOCK, (first + width) // BLOCK):
            block(j)
            step(*AFTER[j])

    log_sum = (logs[:, :128] + logs[:, 128:256]) + (logs[:, 256:384] + logs[:, 384:])
    loss_core[core] = log_sum
    loss_hop = remote(loss_core.at[core], loss_core.at[core], small_send.at[25], small_recv.at[25], partner)
    sent.append(loss_hop)

    top = lax.broadcasted_iota(jnp.int32, (16, 8, CADS), 1) < 4
    first, second = acc[:, 0, :, :], acc[:, 1, :, :]
    sums = jnp.where(
        top,
        first[:, :, :CADS] + pltpu.roll(first[:, :, CADS:], 4, 1),
        pltpu.roll(second[:, :, :CADS], 4, 1) + second[:, :, CADS:],
    )
    cad_part[...] = sums.reshape(NY, 2, 8, CADS)
    across = remote(cad_part.at[:, 1 - core], cad_core, small_send.at[8], small_recv.at[8], partner)
    sent.append(across)

    def exchange(ref, place, first, peers):
        copies = [
            remote(ref.at[place], ref.at[place], small_send.at[first + n], small_recv.at[first + n], peer)
            for n, peer in enumerate(peers)
        ]
        sent.extend(copies)
        return copies

    def arrive(copies):
        for copy in copies:
            copy.wait_recv()

    step(*TAIL[0])
    loss_hop.wait_recv()
    loss_y[y] = loss_core[0] + loss_core[1]
    loss_hops = exchange(loss_y, y, 26, [to_y(d) for d in range(1, NY)])
    across.wait_recv()
    cad_part[:, core] = cad_part[:, core] + cad_core[...]
    cad_from[y] = cad_part[y, core]
    arrivals = [
        remote(cad_part.at[at_y(d), core], cad_from.at[y], small_send.at[8 + d], small_recv.at[8 + d], to_y(d))
        for d in range(1, NY)
    ]
    sent.extend(arrivals)
    step(*TAIL[1])
    arrive(loss_hops)
    loss_x[x] = jnp.sum(loss_y[...], axis=0)
    loss_hops = exchange(loss_x, x, 16, [to_x(d) for d in range(1, NX)])
    step(*TAIL[2])
    arrive(loss_hops)
    loss_z[z] = jnp.sum(loss_x[...], axis=0)
    loss_hops = exchange(loss_z, z, 19, [to_z(d) for d in range(1, NZ - 1)]) + exchange(loss_z, z, 33, [to_z(NZ - 1)])
    step(*TAIL[3])
    arrive(arrivals)
    cad_out[...] = jnp.sum(cad_from[...], axis=0) * cad_scale
    for i in range(len(CHUNKS)):
        wait_for(boxes[i], gather_send.at[i])
    for copy in sent:
        copy.wait_send()
    arrive(loss_hops)
    everything = jnp.sum(loss_z[...], axis=0)
    loss_out[...] = jnp.sum(jnp.sum(everything, axis=0, keepdims=True), axis=1, keepdims=True) * loss_scale
    for _ in range(LEVELS):
        step(*range(len(CHUNKS)))
    for i in range(len(CHUNKS)):
        wait_for(boxes[i], reduce_send.at[i])
    star_out[:, :HALF] = grads[z, x, 0:4, :] * star_scale
    star_out[:, HALF:] = grads[z, x, 4:8, :] * star_scale


def on_device(light, quality, star_factors, cadence_factors):
    stars = light.shape[0] * lax.axis_size("star")
    cads = light.shape[1] * lax.axis_size("cad")
    dma = pltpu.SemaphoreType.DMA
    boxes = [pltpu.VMEM((EDGES, 8, width), F32) for _, width in CHUNKS]
    count = len(CHUNKS)
    hbm = pl.BlockSpec(memory_space=pltpu.HBM)
    vmem = pl.BlockSpec(memory_space=pltpu.VMEM)
    star_gradient, cadence_gradient, loss = pl.pallas_call(
        functools.partial(
            kernel, -1.0 / float(cads) ** 0.5, -1.0 / float(stars) ** 0.5, 2.0 / (float(stars) * float(cads))
        ),
        out_shape=(
            jax.ShapeDtypeStruct((4, 4096), F32),
            jax.ShapeDtypeStruct((8, CADS), F32),
            jax.ShapeDtypeStruct((1, 1), F32),
        ),
        in_specs=[hbm] * 4,
        out_specs=(vmem, vmem, vmem),
        scratch_shapes=[
            pltpu.VMEM((4096, CADS), F32),
            pltpu.VMEM((4, 4096), F32),
            pltpu.VMEM((NZ, NX, 8, HALF), F32),
            pltpu.VMEM((NZ, NX, 8, HALF), F32),
            pltpu.VMEM((NY, 2, 8, CADS), F32),
            pltpu.VMEM((16, 2, 8, 2 * CADS), F32),
            pltpu.VMEM((256, 2 * CADS), BF16),
            pltpu.VMEM((256, 2 * CADS), BF16),
            pltpu.VMEM((1, CADS), jnp.int32),
            pltpu.VMEM((16, 2, 8, 2 * CADS), F32),
            pltpu.VMEM((8, 2 * CADS), F32),
            pltpu.VMEM((NY, 2, 8, CADS), F32),
            pltpu.VMEM((NY, 8, CADS), F32),
            pltpu.VMEM((NY, 8, CADS), F32),
            pltpu.VMEM((2, 8, 128), F32),
            pltpu.VMEM((NY, 8, 128), F32),
            pltpu.VMEM((NX, 8, 128), F32),
            pltpu.VMEM((NZ, 8, 128), F32),
            *boxes,
            dma((4,)),
            dma((count,)), dma((count, LEVELS)), dma((count,)), dma((count, LEVELS)), dma((34,)), dma((34,)),
        ],
        compiler_params=pltpu.CompilerParams(
            collective_id=0, has_side_effects=True, vmem_limit_bytes=40 << 20
        ),
        cost_estimate=pl.CostEstimate(flops=10**9, bytes_accessed=5 * 10**6, transcendentals=2 * 10**6),
        name="cauchy_factor_gradient",
    )(*(
        pltpu.with_memory_space_constraint(array, pltpu.HBM)
        for array in (light, quality.reshape(1, CADS), star_factors.T, cadence_factors.T)
    ))
    return (star_gradient.T, cadence_gradient.T, loss.reshape(()))


def solution(mesh):
    in_specs = (P("star", "cad"), P("cad"), P("star", "cad"), P("cad", "star"))
    out_specs = (P("star", "cad"), P("cad", "star"), P())
    return jax.shard_map(
        on_device, mesh=mesh, in_specs=in_specs, out_specs=out_specs, check_vma=False
    )
```

```python
import functools

import jax
import jax.numpy as jnp
from jax import lax
from jax.experimental import pallas as pl
from jax.experimental.pallas import tpu as pltpu
from jax.sharding import PartitionSpec as P

MESH = pl.DeviceIdType.MESH
F32, BF16 = jnp.float32, jnp.bfloat16
NZ, NX, NY = 8, 4, 8
HALF = 2048
CADS = 256
BLOCK = 256
EDGES = NZ * NX - 1
STEP_Z = (
    (0, 0, 0, 0),
    (1, 1, 0, 1),
    (2, 0, 0, 0),
    (1, 1, 0, 1),
    (-1, -1, 1, 1),
    (-1, -1, 0, -1),
    (-2, 0, 0, 0),
    (-1, 0, -1, -1),
)
STEP_X = (
    (0, 1, -2, -1),
    (0, 0, -1, 0),
    (0, 1, 1, -1),
    (0, 0, -1, -1),
    (0, 0, -1, 0),
    (0, 1, 1, 0),
    (0, 1, 1, -1),
    (0, 1, 0, 0),
)


def tree():
    parents = {
        (dz, dx): ((dz - STEP_Z[dz][dx]) % NZ, (dx - STEP_X[dz][dx]) % NX)
        for dz in range(NZ)
        for dx in range(NX)
        if dz or dx
    }

    def depth(place):
        return 1 + depth(parents[place]) if place in parents else 0

    levels = [[] for _ in range(max(map(depth, parents)))]
    for place, parent in parents.items():
        levels[depth(place) - 1].append((place, parent))
    return levels


TREE = tree()
LEVELS = len(TREE)
CHUNKS = ((0, 512), (512, 512), (1024, 512), (1536, 512))
AFTER = ((), (0,), (), (1,), (), (2, 0), (), (3, 1))
TAIL = ((0, 2), (3, 1, 2, 0), (3, 2, 1, 0), (3, 2, 1, 0))


def split(value):
    high = value.astype(BF16)
    return high, (value - high.astype(F32)).astype(BF16)


def dot3(a, b, dims):
    def one(p, q):
        return lax.dot_general(p, q, (dims, ((), ())), preferred_element_type=F32)

    rows = a[0].shape[0]
    both = one(jnp.concatenate(a, axis=0), b[0])
    return both[:rows] + (one(a[0], b[1]) + both[rows:])


def kernel(
    star_scale, cad_scale, loss_scale,
    light_ref, quality_ref, star_ref, cad_ref,
    star_out, cad_out, loss_out,
    light, own, slabs, grads, cads, expanded, wide_high, wide_low, good, acc, logs,
    cad_part, cad_core, cad_from, loss_core, loss_y, loss_x, loss_z, *rest,
):
    boxes, (sems, gather_send, gather_recv, reduce_send, reduce_recv, small_send, small_recv) = rest[:-7], rest[-7:]
    star, cad = lax.axis_index("star"), lax.axis_index("cad")
    y, core = star // 2, lax.rem(star, 2)
    z, x = cad // NX, lax.rem(cad, NX)

    def at_z(d):
        return lax.rem(z + d + NZ, NZ)

    def at_x(d):
        return lax.rem(x + d + NX, NX)

    def at_y(d):
        return lax.rem(y + d, NY)

    def to_z(d):
        return (star, at_z(d) * NX + x)

    def to_x(d):
        return (star, z * NX + at_x(d))

    def to_y(d):
        return (at_y(d) * 2 + core, cad)

    partner = (y * 2 + 1 - core, cad)

    light_copy = pltpu.make_async_copy(light_ref, light, sems.at[0])
    own_copy = pltpu.make_async_copy(star_ref, own, sems.at[1])
    cad_copy = pltpu.make_async_copy(cad_ref, cads.at[y, core], sems.at[2])
    good_copy = pltpu.make_async_copy(quality_ref, good, sems.at[3])
    own_copy.start()
    cad_copy.start()
    good_copy.start()

    barrier = pltpu.get_barrier_semaphore()
    peers = [to_z(d) for d in range(1, NZ)] + [to_x(d) for d in range(1, NX)]
    peers += [to_y(d) for d in range(1, NY)] + [partner]
    slants = {(a, b) for row in zip(STEP_Z, STEP_X) for a, b in zip(*row) if a and b}
    slants |= {(-a, -b) for a, b in slants}
    peers += [(star, at_z(a) * NX + at_x(b)) for a, b in sorted(slants)]
    for peer in peers:
        pl.semaphore_signal(barrier, inc=1, device_id=peer, device_id_type=MESH)
    own_copy.wait()
    slabs[z, x, 0:4, :] = own[:, :HALF]
    slabs[z, x, 4:8, :] = own[:, HALF:]
    pl.semaphore_wait(barrier, len(peers))

    def remote(src, dst, send, recv, where):
        copy = pltpu.make_async_remote_copy(
            src_ref=src, dst_ref=dst, send_sem=send, recv_sem=recv,
            device_id=where, device_id_type=MESH,
        )
        copy.start()
        return copy

    sent = []

    def whole(offset):
        return (at_z(offset[0]), at_x(offset[1]))

    def minus(a, b=(0, 0)):
        return (b[0] - a[0], b[1] - a[1])

    def device(offset):
        places = whole(offset)
        return (star, places[0] * NX + places[1])

    def wait_for(ref, semaphore):
        pltpu.make_async_copy(ref, ref, semaphore).wait()

    def gather_rounds(index, first, width):
        columns = pl.ds(first, width)
        for level, edges in enumerate(TREE):
            if level:
                wait_for(boxes[index].at[:len(TREE[level - 1])], gather_recv.at[index, level - 1])
            for offset, parent in edges:
                slab = slabs.at[whole(minus(parent))].at[:, columns]
                remote(
                    slab, slab, gather_send.at[index], gather_recv.at[index, level], device(minus(parent, offset))
                )
            yield False
        wait_for(boxes[index].at[:len(TREE[-1])], gather_recv.at[index, LEVELS - 1])

    def reduce_rounds(index, first, width):
        columns = pl.ds(first, width)
        box = boxes[index]
        starts = [sum(len(edges) for edges in TREE[:level]) for level in range(LEVELS)]

        def gathered(offset, level):
            mine = grads.at[whole(minus(offset))].at[:, columns]
            total = None
            for n, (_, parent) in enumerate(TREE[level] if level < LEVELS else ()):
                if parent == offset:
                    n += starts[level]
                    total = box[n] if total is None else total + box[n]
            if total is not None:
                mine[...] = mine[...] + total
            return mine

        def landed(level):
            if level < LEVELS:
                wait_for(box.at[pl.ds(starts[level], len(TREE[level]))], reduce_recv.at[index, level])

        for level in reversed(range(LEVELS)):
            landed(level + 1)
            for n, (offset, parent) in enumerate(TREE[level]):
                remote(
                    gathered(offset, level + 1), box.at[starts[level] + n], reduce_send.at[index],
                    reduce_recv.at[index, level], device(minus(offset, parent)),
                )
            yield False
        landed(0)
        gathered((0, 0), 0)

    cad_copy.wait()
    cad_in = [
        remote(cads.at[y, core], cads.at[y, core], small_send.at[d - 1], small_recv.at[d - 1], to_y(d))
        for d in range(1, NY)
    ]
    sent.extend(cad_in)
    gathers = [gather_rounds(i, *chunk) for i, chunk in enumerate(CHUNKS)]
    reduces = [reduce_rounds(i, *chunk) for i, chunk in enumerate(CHUNKS)]

    def advance(rounds):
        for g in tuple(rounds):
            if next(g, True):
                rounds.remove(g)

    advance(list(gathers))
    light_copy.start()
    ahead, others = gathers[:1], gathers[1:]
    advance(list(ahead))
    advance(list(others))
    advance(list(ahead))
    for copy in cad_in:
        copy.wait_recv()
    cad_across = remote(cads.at[:, core], cads.at[:, core], small_send.at[7], small_recv.at[7], partner)
    sent.append(cad_across)
    advance(list(others))
    advance(list(ahead))
    cad_across.wait_recv()

    good_copy.wait()
    keep = good[...].astype(F32)
    values = cads[...].reshape(16, 8, CADS) * keep[None]
    turned = pltpu.roll(values, 4, 1)
    upper = lax.broadcasted_iota(jnp.int32, (16, 8, CADS), 1) < 4
    zero = jnp.zeros_like(values)
    expanded[:, 0, :, :CADS] = jnp.where(upper, values, zero)
    expanded[:, 1, :, :CADS] = jnp.where(upper, turned, zero)
    expanded[:, 0, :, CADS:] = jnp.where(upper, zero, turned)
    expanded[:, 1, :, CADS:] = jnp.where(upper, zero, values)
    high, low = split(expanded[...].reshape(256, 2 * CADS))
    wide_high[...] = high
    wide_low[...] = low
    acc[...] = jnp.zeros_like(acc)
    logs[...] = jnp.zeros_like(logs)

    for _ in range(3, LEVELS):
        advance(list(others))
        advance(list(ahead))
    light_copy.wait()

    def block(j):
        columns = pl.ds(j * BLOCK, BLOCK)
        loads = slabs[:, :, :, columns].reshape(256, BLOCK)
        wide = (wide_high[...], wide_low[...])
        predicted = dot3(split(loads.T), wide, ((1,), (0,)))
        keep = good[...].astype(F32)
        weighted = []
        for half in range(2):
            rows = pl.ds(half * HALF + j * BLOCK, BLOCK)
            side = slice(half * CADS, (half + 1) * CADS)
            residual = light[rows, :] * keep - predicted[:, side]
            ratio = 1.0 + (residual * 0.5) ** 2
            weighted.append(residual * pl.reciprocal(ratio))
            four = ratio.reshape(4, BLOCK // 4, CADS)
            four = (four[0] * four[1]) * (four[2] * four[3])
            logs[:, side] += jnp.sum(jnp.log(four).reshape(BLOCK // 32, 8, CADS), axis=0)
        weighted = split(jnp.concatenate(weighted, axis=1))
        grads[:, :, :, columns] = dot3(wide, weighted, ((1,), (1,))).reshape(NZ, NX, 8, BLOCK)
        acc[...] += dot3(split(loads), weighted, ((1,), (0,))).reshape(acc.shape)

    def step(*which):
        for i in which:
            next(reduces[i], None)

    for i, (first, width) in enumerate(CHUNKS):
        next(gathers[i], None)
        for j in range(first // BLOCK, (first + width) // BLOCK):
            block(j)
            step(*AFTER[j])

    log_sum = (logs[:, :128] + logs[:, 128:256]) + (logs[:, 256:384] + logs[:, 384:])
    loss_core[core] = log_sum
    loss_hop = remote(loss_core.at[core], loss_core.at[core], small_send.at[25], small_recv.at[25], partner)
    sent.append(loss_hop)

    top = lax.broadcasted_iota(jnp.int32, (16, 8, CADS), 1) < 4
    first, second = acc[:, 0, :, :], acc[:, 1, :, :]
    sums = jnp.where(
        top,
        first[:, :, :CADS] + pltpu.roll(first[:, :, CADS:], 4, 1),
        pltpu.roll(second[:, :, :CADS], 4, 1) + second[:, :, CADS:],
    )
    cad_part[...] = sums.reshape(NY, 2, 8, CADS)
    across = remote(cad_part.at[:, 1 - core], cad_core, small_send.at[8], small_recv.at[8], partner)
    sent.append(across)

    def exchange(ref, place, first, peers):
        copies = [
            remote(ref.at[place], ref.at[place], small_send.at[first + n], small_recv.at[first + n], peer)
            for n, peer in enumerate(peers)
        ]
        sent.extend(copies)
        return copies

    def arrive(copies):
        for copy in copies:
            copy.wait_recv()

    step(*TAIL[0])
    loss_hop.wait_recv()
    loss_y[y] = loss_core[0] + loss_core[1]
    loss_hops = exchange(loss_y, y, 26, [to_y(d) for d in range(1, NY)])
    across.wait_recv()
    cad_part[:, core] = cad_part[:, core] + cad_core[...]
    cad_from[y] = cad_part[y, core]
    arrivals = [
        remote(cad_part.at[at_y(d), core], cad_from.at[y], small_send.at[8 + d], small_recv.at[8 + d], to_y(d))
        for d in range(1, NY)
    ]
    sent.extend(arrivals)
    step(*TAIL[1])
    arrive(loss_hops)
    loss_x[x] = jnp.sum(loss_y[...], axis=0)
    loss_hops = exchange(loss_x, x, 16, [to_x(d) for d in range(1, NX)])
    step(*TAIL[2])
    arrive(loss_hops)
    loss_z[z] = jnp.sum(loss_x[...], axis=0)
    loss_hops = exchange(loss_z, z, 19, [to_z(d) for d in range(1, NZ - 1)]) + exchange(loss_z, z, 33, [to_z(NZ - 1)])
    step(*TAIL[3])
    arrive(arrivals)
    cad_out[...] = jnp.sum(cad_from[...], axis=0) * cad_scale
    for i in range(len(CHUNKS)):
        wait_for(boxes[i], gather_send.at[i])
    for copy in sent:
        copy.wait_send()
    arrive(loss_hops)
    everything = jnp.sum(loss_z[...], axis=0)
    loss_out[...] = jnp.sum(jnp.sum(everything, axis=0, keepdims=True), axis=1, keepdims=True) * loss_scale
    for _ in range(LEVELS):
        step(*range(len(CHUNKS)))
    for i in range(len(CHUNKS)):
        wait_for(boxes[i], reduce_send.at[i])
    star_out[:, :HALF] = grads[z, x, 0:4, :] * star_scale
    star_out[:, HALF:] = grads[z, x, 4:8, :] * star_scale


def on_device(light, quality, star_factors, cadence_factors):
    stars = light.shape[0] * lax.axis_size("star")
    cads = light.shape[1] * lax.axis_size("cad")
    dma = pltpu.SemaphoreType.DMA
    boxes = [pltpu.VMEM((EDGES, 8, width), F32) for _, width in CHUNKS]
    count = len(CHUNKS)
    hbm = pl.BlockSpec(memory_space=pltpu.HBM)
    vmem = pl.BlockSpec(memory_space=pltpu.VMEM)
    star_gradient, cadence_gradient, loss = pl.pallas_call(
        functools.partial(
            kernel, -1.0 / float(cads) ** 0.5, -1.0 / float(stars) ** 0.5, 2.0 / (float(stars) * float(cads))
        ),
        out_shape=(
            jax.ShapeDtypeStruct((4, 4096), F32),
            jax.ShapeDtypeStruct((8, CADS), F32),
            jax.ShapeDtypeStruct((1, 1), F32),
        ),
        in_specs=[hbm] * 4,
        out_specs=(vmem, vmem, vmem),
        scratch_shapes=[
            pltpu.VMEM((4096, CADS), F32),
            pltpu.VMEM((4, 4096), F32),
            pltpu.VMEM((NZ, NX, 8, HALF), F32),
            pltpu.VMEM((NZ, NX, 8, HALF), F32),
            pltpu.VMEM((NY, 2, 8, CADS), F32),
            pltpu.VMEM((16, 2, 8, 2 * CADS), F32),
            pltpu.VMEM((256, 2 * CADS), BF16),
            pltpu.VMEM((256, 2 * CADS), BF16),
            pltpu.VMEM((1, CADS), jnp.int32),
            pltpu.VMEM((16, 2, 8, 2 * CADS), F32),
            pltpu.VMEM((8, 2 * CADS), F32),
            pltpu.VMEM((NY, 2, 8, CADS), F32),
            pltpu.VMEM((NY, 8, CADS), F32),
            pltpu.VMEM((NY, 8, CADS), F32),
            pltpu.VMEM((2, 8, 128), F32),
            pltpu.VMEM((NY, 8, 128), F32),
            pltpu.VMEM((NX, 8, 128), F32),
            pltpu.VMEM((NZ, 8, 128), F32),
            *boxes,
            dma((4,)),
            dma((count,)), dma((count, LEVELS)), dma((count,)), dma((count, LEVELS)), dma((34,)), dma((34,)),
        ],
        compiler_params=pltpu.CompilerParams(
            collective_id=0, has_side_effects=True, vmem_limit_bytes=40 << 20
        ),
        cost_estimate=pl.CostEstimate(flops=10**9, bytes_accessed=5 * 10**6, transcendentals=2 * 10**6),
        name="cauchy_factor_gradient",
    )(*(
        pltpu.with_memory_space_constraint(array, pltpu.HBM)
        for array in (light, quality.reshape(1, CADS), star_factors.T, cadence_factors.T)
    ))
    return (star_gradient.T, cadence_gradient.T, loss.reshape(()))


def solution(mesh):
    in_specs = (P("star", "cad"), P("cad"), P("star", "cad"), P("cad", "star"))
    out_specs = (P("star", "cad"), P("cad", "star"), P())
    return jax.shard_map(
        on_device, mesh=mesh, in_specs=in_specs, out_specs=out_specs, check_vma=False
    )
```

```python
import functools

import jax
import jax.numpy as jnp
from jax import lax
from jax.experimental import pallas as pl
from jax.experimental.pallas import tpu as pltpu
from jax.sharding import PartitionSpec as P

MESH = pl.DeviceIdType.MESH
F32, BF16 = jnp.float32, jnp.bfloat16
NZ, NX, NY = 8, 4, 8
HALF = 2048
CADS = 256
BLOCK = 256
EDGES = NZ * NX - 1
STEP_Z = (
    (0, 0, 0, 0),
    (1, 1, 0, 1),
    (2, 0, 0, 0),
    (1, 1, 0, 1),
    (-1, -1, 1, 1),
    (-1, -1, 0, -1),
    (-2, 0, 0, 0),
    (-1, 0, -1, -1),
)
STEP_X = (
    (0, 1, -2, -1),
    (0, 0, -1, 0),
    (0, 1, 1, -1),
    (0, 0, -1, -1),
    (0, 0, -1, 0),
    (0, 1, 1, 0),
    (0, 1, 1, -1),
    (0, 1, 0, 0),
)


SPREAD_Z = (
    (0, 0, 0, 0),
    (1, 0, 0, 0),
    (1, 1, 1, 0),
    (2, 0, 0, 0),
    (1, 1, -2, 0),
    (-1, -1, 0, 0),
    (-1, -2, 0, 0),
    (-1, 0, -1, 0),
)
SPREAD_X = (
    (0, 1, -1, -1),
    (0, 1, 1, -1),
    (0, 0, 0, -1),
    (0, 1, 1, -1),
    (0, 0, 0, -1),
    (0, 0, 1, -1),
    (0, 0, 1, -1),
    (0, 1, 0, -1),
)


def tree(step_z, step_x):
    parents = {
        (dz, dx): ((dz - step_z[dz][dx]) % NZ, (dx - step_x[dz][dx]) % NX)
        for dz in range(NZ)
        for dx in range(NX)
        if dz or dx
    }

    def depth(place):
        return 1 + depth(parents[place]) if place in parents else 0

    levels = [[] for _ in range(max(map(depth, parents)))]
    for place, parent in parents.items():
        levels[depth(place) - 1].append((place, parent))
    return levels


TREE, SPREAD = tree(STEP_Z, STEP_X), tree(SPREAD_Z, SPREAD_X)
LEVELS = len(TREE)
CHUNKS = ((0, 512), (512, 512), (1024, 512), (1536, 512))
AFTER = ((), (0,), (), (1,), (), (2, 0), (), (3, 1))
TAIL = ((0, 2), (3, 1, 2, 0), (3, 2, 1, 0), (3, 2, 1, 0))


def split(value):
    high = value.astype(BF16)
    return high, (value - high.astype(F32)).astype(BF16)


def dot3(a, b, dims):
    def one(p, q):
        return lax.dot_general(p, q, (dims, ((), ())), preferred_element_type=F32)

    rows = a[0].shape[0]
    both = one(jnp.concatenate(a, axis=0), b[0])
    return both[:rows] + (one(a[0], b[1]) + both[rows:])


def kernel(
    star_scale, cad_scale, loss_scale,
    light_ref, quality_ref, star_ref, cad_ref,
    star_out, cad_out, loss_out,
    light, own, slabs, grads, cads, expanded, wide_high, wide_low, good, acc, logs,
    cad_part, cad_core, cad_from, loss_core, loss_y, loss_x, loss_z, *rest,
):
    boxes, (sems, gather_send, gather_recv, reduce_send, reduce_recv, small_send, small_recv) = rest[:-7], rest[-7:]
    star, cad = lax.axis_index("star"), lax.axis_index("cad")
    y, core = star // 2, lax.rem(star, 2)
    z, x = cad // NX, lax.rem(cad, NX)

    def at_z(d):
        return lax.rem(z + d + NZ, NZ)

    def at_x(d):
        return lax.rem(x + d + NX, NX)

    def at_y(d):
        return lax.rem(y + d, NY)

    def to_z(d):
        return (star, at_z(d) * NX + x)

    def to_x(d):
        return (star, z * NX + at_x(d))

    def to_y(d):
        return (at_y(d) * 2 + core, cad)

    partner = (y * 2 + 1 - core, cad)

    light_copy = pltpu.make_async_copy(light_ref, light, sems.at[0])
    own_copy = pltpu.make_async_copy(star_ref, own, sems.at[1])
    cad_copy = pltpu.make_async_copy(cad_ref, cads.at[y, core], sems.at[2])
    good_copy = pltpu.make_async_copy(quality_ref, good, sems.at[3])
    own_copy.start()
    cad_copy.start()
    good_copy.start()

    barrier = pltpu.get_barrier_semaphore()
    peers = [to_z(d) for d in range(1, NZ)] + [to_x(d) for d in range(1, NX)]
    peers += [to_y(d) for d in range(1, NY)] + [partner]
    slants = {(a, b) for row in zip(STEP_Z, STEP_X) for a, b in zip(*row) if a and b}
    slants |= {(-a, -b) for a, b in slants}
    peers += [(star, at_z(a) * NX + at_x(b)) for a, b in sorted(slants)]
    for peer in peers:
        pl.semaphore_signal(barrier, inc=1, device_id=peer, device_id_type=MESH)
    own_copy.wait()
    slabs[z, x, 0:4, :] = own[:, :HALF]
    slabs[z, x, 4:8, :] = own[:, HALF:]
    pl.semaphore_wait(barrier, len(peers))

    def remote(src, dst, send, recv, where):
        copy = pltpu.make_async_remote_copy(
            src_ref=src, dst_ref=dst, send_sem=send, recv_sem=recv,
            device_id=where, device_id_type=MESH,
        )
        copy.start()
        return copy

    sent = []

    def whole(offset):
        return (at_z(offset[0]), at_x(offset[1]))

    def minus(a, b=(0, 0)):
        return (b[0] - a[0], b[1] - a[1])

    def device(offset):
        places = whole(offset)
        return (star, places[0] * NX + places[1])

    def wait_for(ref, semaphore):
        pltpu.make_async_copy(ref, ref, semaphore).wait()

    def gather_rounds(index, first, width):
        columns = pl.ds(first, width)
        for level, edges in enumerate(SPREAD):
            if level:
                wait_for(boxes[index].at[:len(SPREAD[level - 1])], gather_recv.at[index, level - 1])
            for offset, parent in edges:
                slab = slabs.at[whole(minus(parent))].at[:, columns]
                remote(
                    slab, slab, gather_send.at[index], gather_recv.at[index, level], device(minus(parent, offset))
                )
            yield False
        wait_for(boxes[index].at[:len(SPREAD[-1])], gather_recv.at[index, len(SPREAD) - 1])

    def reduce_rounds(index, first, width):
        columns = pl.ds(first, width)
        box = boxes[index]
        starts = [sum(len(edges) for edges in TREE[:level]) for level in range(LEVELS)]

        def gathered(offset, level):
            mine = grads.at[whole(minus(offset))].at[:, columns]
            total = None
            for n, (_, parent) in enumerate(TREE[level] if level < LEVELS else ()):
                if parent == offset:
                    n += starts[level]
                    total = box[n] if total is None else total + box[n]
            if total is not None:
                mine[...] = mine[...] + total
            return mine

        def landed(level):
            if level < LEVELS:
                wait_for(box.at[pl.ds(starts[level], len(TREE[level]))], reduce_recv.at[index, level])

        for level in reversed(range(LEVELS)):
            landed(level + 1)
            for n, (offset, parent) in enumerate(TREE[level]):
                remote(
                    gathered(offset, level + 1), box.at[starts[level] + n], reduce_send.at[index],
                    reduce_recv.at[index, level], device(minus(offset, parent)),
                )
            yield False
        landed(0)
        gathered((0, 0), 0)

    cad_copy.wait()
    cad_in = [
        remote(cads.at[y, core], cads.at[y, core], small_send.at[d - 1], small_recv.at[d - 1], to_y(d))
        for d in range(1, NY)
    ]
    sent.extend(cad_in)
    gathers = [gather_rounds(i, *chunk) for i, chunk in enumerate(CHUNKS)]
    reduces = [reduce_rounds(i, *chunk) for i, chunk in enumerate(CHUNKS)]

    def advance(rounds):
        for g in tuple(rounds):
            if next(g, True):
                rounds.remove(g)

    advance(list(gathers))
    light_copy.start()
    ahead, others = gathers[:1], gathers[1:]
    advance(list(ahead))
    advance(list(others))
    advance(list(ahead))
    for copy in cad_in:
        copy.wait_recv()
    cad_across = remote(cads.at[:, core], cads.at[:, core], small_send.at[7], small_recv.at[7], partner)
    sent.append(cad_across)
    advance(list(others))
    advance(list(ahead))
    cad_across.wait_recv()

    good_copy.wait()
    keep = good[...].astype(F32)
    values = cads[...].reshape(16, 8, CADS) * keep[None]
    turned = pltpu.roll(values, 4, 1)
    upper = lax.broadcasted_iota(jnp.int32, (16, 8, CADS), 1) < 4
    zero = jnp.zeros_like(values)
    expanded[:, 0, :, :CADS] = jnp.where(upper, values, zero)
    expanded[:, 1, :, :CADS] = jnp.where(upper, turned, zero)
    expanded[:, 0, :, CADS:] = jnp.where(upper, zero, turned)
    expanded[:, 1, :, CADS:] = jnp.where(upper, zero, values)
    high, low = split(expanded[...].reshape(256, 2 * CADS))
    wide_high[...] = high
    wide_low[...] = low
    acc[...] = jnp.zeros_like(acc)
    logs[...] = jnp.zeros_like(logs)

    for _ in range(3, len(SPREAD)):
        advance(list(others))
        advance(list(ahead))
    light_copy.wait()

    def block(j):
        columns = pl.ds(j * BLOCK, BLOCK)
        loads = slabs[:, :, :, columns].reshape(256, BLOCK)
        wide = (wide_high[...], wide_low[...])
        predicted = dot3(split(loads.T), wide, ((1,), (0,)))
        keep = good[...].astype(F32)
        weighted = []
        for half in range(2):
            rows = pl.ds(half * HALF + j * BLOCK, BLOCK)
            side = slice(half * CADS, (half + 1) * CADS)
            residual = light[rows, :] * keep - predicted[:, side]
            ratio = 1.0 + (residual * 0.5) ** 2
            weighted.append(residual * pl.reciprocal(ratio))
            four = ratio.reshape(4, BLOCK // 4, CADS)
            four = (four[0] * four[1]) * (four[2] * four[3])
            logs[:, side] += jnp.sum(jnp.log(four).reshape(BLOCK // 32, 8, CADS), axis=0)
        weighted = split(jnp.concatenate(weighted, axis=1))
        grads[:, :, :, columns] = dot3(wide, weighted, ((1,), (1,))).reshape(NZ, NX, 8, BLOCK)
        acc[...] += dot3(split(loads), weighted, ((1,), (0,))).reshape(acc.shape)

    def step(*which):
        for i in which:
            next(reduces[i], None)

    for i, (first, width) in enumerate(CHUNKS):
        next(gathers[i], None)
        for j in range(first // BLOCK, (first + width) // BLOCK):
            block(j)
            step(*AFTER[j])

    log_sum = (logs[:, :128] + logs[:, 128:256]) + (logs[:, 256:384] + logs[:, 384:])
    loss_core[core] = log_sum
    loss_hop = remote(loss_core.at[core], loss_core.at[core], small_send.at[25], small_recv.at[25], partner)
    sent.append(loss_hop)

    top = lax.broadcasted_iota(jnp.int32, (16, 8, CADS), 1) < 4
    first, second = acc[:, 0, :, :], acc[:, 1, :, :]
    sums = jnp.where(
        top,
        first[:, :, :CADS] + pltpu.roll(first[:, :, CADS:], 4, 1),
        pltpu.roll(second[:, :, :CADS], 4, 1) + second[:, :, CADS:],
    )
    cad_part[...] = sums.reshape(NY, 2, 8, CADS)
    across = remote(cad_part.at[:, 1 - core], cad_core, small_send.at[8], small_recv.at[8], partner)
    sent.append(across)

    def exchange(ref, place, first, peers):
        copies = [
            remote(ref.at[place], ref.at[place], small_send.at[first + n], small_recv.at[first + n], peer)
            for n, peer in enumerate(peers)
        ]
        sent.extend(copies)
        return copies

    def arrive(copies):
        for copy in copies:
            copy.wait_recv()

    step(*TAIL[0])
    loss_hop.wait_recv()
    loss_y[y] = loss_core[0] + loss_core[1]
    loss_hops = exchange(loss_y, y, 26, [to_y(d) for d in range(1, NY)])
    across.wait_recv()
    cad_part[:, core] = cad_part[:, core] + cad_core[...]
    cad_from[y] = cad_part[y, core]
    arrivals = [
        remote(cad_part.at[at_y(d), core], cad_from.at[y], small_send.at[8 + d], small_recv.at[8 + d], to_y(d))
        for d in range(1, NY)
    ]
    sent.extend(arrivals)
    step(*TAIL[1])
    arrive(loss_hops)
    loss_x[x] = jnp.sum(loss_y[...], axis=0)
    loss_hops = exchange(loss_x, x, 16, [to_x(d) for d in range(1, NX)])
    step(*TAIL[2])
    arrive(loss_hops)
    loss_z[z] = jnp.sum(loss_x[...], axis=0)
    loss_hops = exchange(loss_z, z, 19, [to_z(d) for d in range(1, NZ - 1)]) + exchange(loss_z, z, 33, [to_z(NZ - 1)])
    step(*TAIL[3])
    arrive(arrivals)
    cad_out[...] = jnp.sum(cad_from[...], axis=0) * cad_scale
    for i in range(len(CHUNKS)):
        wait_for(boxes[i], gather_send.at[i])
    for copy in sent:
        copy.wait_send()
    arrive(loss_hops)
    everything = jnp.sum(loss_z[...], axis=0)
    loss_out[...] = jnp.sum(jnp.sum(everything, axis=0, keepdims=True), axis=1, keepdims=True) * loss_scale
    for _ in range(LEVELS):
        step(*range(len(CHUNKS)))
    for i in range(len(CHUNKS)):
        wait_for(boxes[i], reduce_send.at[i])
    star_out[:, :HALF] = grads[z, x, 0:4, :] * star_scale
    star_out[:, HALF:] = grads[z, x, 4:8, :] * star_scale


def on_device(light, quality, star_factors, cadence_factors):
    stars = light.shape[0] * lax.axis_size("star")
    cads = light.shape[1] * lax.axis_size("cad")
    dma = pltpu.SemaphoreType.DMA
    boxes = [pltpu.VMEM((EDGES, 8, width), F32) for _, width in CHUNKS]
    count = len(CHUNKS)
    hbm = pl.BlockSpec(memory_space=pltpu.HBM)
    vmem = pl.BlockSpec(memory_space=pltpu.VMEM)
    star_gradient, cadence_gradient, loss = pl.pallas_call(
        functools.partial(
            kernel, -1.0 / float(cads) ** 0.5, -1.0 / float(stars) ** 0.5, 2.0 / (float(stars) * float(cads))
        ),
        out_shape=(
            jax.ShapeDtypeStruct((4, 4096), F32),
            jax.ShapeDtypeStruct((8, CADS), F32),
            jax.ShapeDtypeStruct((1, 1), F32),
        ),
        in_specs=[hbm] * 4,
        out_specs=(vmem, vmem, vmem),
        scratch_shapes=[
            pltpu.VMEM((4096, CADS), F32),
            pltpu.VMEM((4, 4096), F32),
            pltpu.VMEM((NZ, NX, 8, HALF), F32),
            pltpu.VMEM((NZ, NX, 8, HALF), F32),
            pltpu.VMEM((NY, 2, 8, CADS), F32),
            pltpu.VMEM((16, 2, 8, 2 * CADS), F32),
            pltpu.VMEM((256, 2 * CADS), BF16),
            pltpu.VMEM((256, 2 * CADS), BF16),
            pltpu.VMEM((1, CADS), jnp.int32),
            pltpu.VMEM((16, 2, 8, 2 * CADS), F32),
            pltpu.VMEM((8, 2 * CADS), F32),
            pltpu.VMEM((NY, 2, 8, CADS), F32),
            pltpu.VMEM((NY, 8, CADS), F32),
            pltpu.VMEM((NY, 8, CADS), F32),
            pltpu.VMEM((2, 8, 128), F32),
            pltpu.VMEM((NY, 8, 128), F32),
            pltpu.VMEM((NX, 8, 128), F32),
            pltpu.VMEM((NZ, 8, 128), F32),
            *boxes,
            dma((4,)),
            dma((count,)), dma((count, len(SPREAD))), dma((count,)), dma((count, LEVELS)), dma((34,)), dma((34,)),
        ],
        compiler_params=pltpu.CompilerParams(
            collective_id=0, has_side_effects=True, vmem_limit_bytes=40 << 20
        ),
        cost_estimate=pl.CostEstimate(flops=10**9, bytes_accessed=5 * 10**6, transcendentals=2 * 10**6),
        name="cauchy_factor_gradient",
    )(*(
        pltpu.with_memory_space_constraint(array, pltpu.HBM)
        for array in (light, quality.reshape(1, CADS), star_factors.T, cadence_factors.T)
    ))
    return (star_gradient.T, cadence_gradient.T, loss.reshape(()))


def solution(mesh):
    in_specs = (P("star", "cad"), P("cad"), P("star", "cad"), P("cad", "star"))
    out_specs = (P("star", "cad"), P("cad", "star"), P())
    return jax.shard_map(
        on_device, mesh=mesh, in_specs=in_specs, out_specs=out_specs, check_vma=False
    )
```
